32 devices in a mesh: freq: 2 (over y), harm: 4 (over z), wall: 4 (over x, core).
Axes of the slice: x: 2, y: 2, z: 4, core: 2. Of those that a mesh axis runs over, the one named last changes fastest.
Arguments:
- sketch: bfloat16 [32, 1024, 128], P(('freq', 'harm'), 'wall'), parts along dimension 0, may hold values from -48 to 48
- inverse_blocks: bfloat16 [32, 1024, 1024], P(('freq', 'harm'), 'wall'), parts along dimension 0, may hold values from -0.1875 to 0.1875
- couple_up: bfloat16 [8, 1024, 1024], P('freq', 'wall'), parts along dimension 0, may hold values from -0.03125 to 0.03125
- couple_down: bfloat16 [8, 1024, 1024], P('freq', 'wall'), parts along dimension 0, may hold values from -0.03125 to 0.03125
- strip_harmonics: int32 [8], P('freq'), parts along dimension 0, may hold values from 0 to 3
Outputs:
- basis: float32 [32, 1024, 128], P(('freq', 'harm'), 'wall'), parts along dimension 0
- triangle: float32 [256, 128], P('freq'), parts along dimension 0
The draws below stay inside these ranges and needn't reach their ends.
There are 2 independent parts, one for each index of `freq`. The reference program is written for one: setup_inputs(seed, part) draws one part's arguments, and reference() takes and returns one part's arrays. A program takes and returns all parts, laid end to end along the dimension named above; each array names one. Nothing has to cross between parts.
Inputs may be any that keep to these rules, and one draw needn't show every extreme that they name: `strip_harmonics`: each entry one of 0 to 3; entries may repeat.
All inputs are finite; a program needn't handle non-finite values.
Results may differ from the reference program's by a relative error of at most 0.0045.
Values may be sent and summed in bfloat16 or wider, within the bound.
A program may use at most 64 MiB of HBM per device.

```python
import math
import jax
import jax.numpy as jnp
from jax import lax

ROWS = 1024
COLUMNS = 128
BAND = 4
SWEEPS = 3
HARMONICS = 16


def draw_sketch(key, part):
    scale_key = jax.random.fold_in(key, 7101)
    entry_key = jax.random.fold_in(key, 7102)
    levels = jax.random.uniform(scale_key, (HARMONICS, 1, 1), jnp.float32, 0.0, math.log(8.0))
    amplitude = jnp.exp(levels)
    entries = jnp.clip(jax.random.normal(entry_key, (HARMONICS, ROWS, COLUMNS), jnp.float32), -6.0, 6.0)
    return (entries * amplitude).astype(jnp.bfloat16)


def place_ends(drawn, rng, smallest, largest):
    index_at = [jax.random.randint(jax.random.fold_in(rng, axis), (), 0, length) for axis, length in enumerate(drawn.shape)]
    longest = drawn.shape.index(max(drawn.shape))
    next_to = index_at[:longest] + [(index_at[longest] + 1) % drawn.shape[longest]] + index_at[longest + 1:]
    return drawn.at[tuple(index_at)].set(smallest).at[tuple(next_to)].set(largest)


def level_of(own_key, dims, split, smallest, largest):
    gain = 1.0
    for axis_at, shards_of in split:
        heights = jax.random.uniform(jax.random.fold_in(jax.random.fold_in(own_key, 6), axis_at), (shards_of,), jnp.float32, smallest / len(split), largest / len(split))
        gain = gain * jnp.repeat(jnp.exp(heights), dims[axis_at] // shards_of).reshape((-1,) + (1,) * (len(dims) - 1 - axis_at))
    return gain


def gaussian(key, dims, width, reach, split=(), held_as=jnp.bfloat16):
    level = level_of(key, dims, split, -0.22, 0.18) if split else 1.0
    values = jax.random.normal(key, dims, jnp.float32) * width * level
    return jnp.minimum(jnp.maximum(values, -reach), reach).astype(held_as)


def setup_inputs(seed: int = 0, part: int = 0) -> dict:
    splits = jax.random.split(jax.random.key(seed), 6)
    part_keys = jax.random.split(jax.random.fold_in(splits[5], part), 6)
    sketch = draw_sketch(jax.random.fold_in(jax.random.fold_in(splits[5], part), 71), part)
    inverse_blocks = gaussian(part_keys[1], (HARMONICS, ROWS, ROWS), ROWS ** -0.5, 0.1875, ((0, 4), (1, 4)))
    couple_up = gaussian(part_keys[2], (BAND, ROWS, ROWS), (32 * ROWS) ** -0.5, 0.03125, ((1, 4),))
    couple_down = gaussian(part_keys[3], (BAND, ROWS, ROWS), (32 * ROWS) ** -0.5, 0.03125, ((1, 4),))
    strip_harmonics = place_ends(jax.random.randint(part_keys[4], (BAND,), 0, BAND), jax.random.fold_in(part_keys[4], 1), 0, BAND - 1).astype(jnp.int32)
    return {"sketch": sketch, "inverse_blocks": inverse_blocks, "couple_up": couple_up, "couple_down": couple_down, "strip_harmonics": strip_harmonics}


def reference(sketch, inverse_blocks, couple_up, couple_down, strip_harmonics):
    offsets = (strip_harmonics + 1).astype(jnp.int32)
    inverse_wide = inverse_blocks.astype(jnp.float32)
    up_wide = couple_up.astype(jnp.float32)
    down_wide = couple_down.astype(jnp.float32)
    sketch_wide = sketch.astype(jnp.float32)
    positions = jnp.arange(HARMONICS, dtype=jnp.int32)

    def apply_inverse(source):
        return jnp.einsum('hrc,hck->hrk', inverse_wide, source.astype(jnp.float32))
    state = apply_inverse(sketch).astype(jnp.bfloat16)
    sampled = None
    for sweep in range(SWEEPS):
        coupled = jnp.zeros((HARMONICS, ROWS, COLUMNS), jnp.float32)
        state_wide = state.astype(jnp.float32)
        for j in range(BAND):
            below = jnp.take(state_wide, (positions - offsets[j]) % HARMONICS, axis=0)
            above = jnp.take(state_wide, (positions + offsets[j]) % HARMONICS, axis=0)
            coupled = coupled + jnp.einsum('rc,hck->hrk', up_wide[j], below)
            coupled = coupled + jnp.einsum('rc,hck->hrk', down_wide[j], above)
        rhs = (sketch_wide - coupled).astype(jnp.bfloat16)
        result = apply_inverse(rhs)
        if sweep < SWEEPS - 1:
            state = result.astype(jnp.bfloat16)
        else:
            sampled = result
    flat = sampled.reshape(HARMONICS * ROWS, COLUMNS)
    count = HARMONICS * ROWS
    gram = jnp.dot(flat.T.astype(jnp.float32), flat.astype(jnp.float32), precision=lax.Precision.HIGHEST, preferred_element_type=jnp.float32) / count
    lower = jnp.linalg.cholesky(gram)
    basis = jax.scipy.linalg.solve_triangular(lower, flat.T, lower=True).T
    triangle = lower.T
    return (basis.reshape(HARMONICS, ROWS, COLUMNS), triangle)
```

```python
import functools

import jax
import jax.numpy as jnp
from jax import lax
from jax.experimental import pallas as pl
from jax.experimental.pallas import tpu as pltpu
from jax.sharding import PartitionSpec as P

BAND = 4
SWEEPS = 3
MESH = pl.DeviceIdType.MESH


def flip(index, bit):
    return index + bit - 2 * bit * (lax.div(index, bit) % 2)


def bits_of(count):
    return [1 << b for b in range(count.bit_length() - 1)]


def visit_order(count):
    order = []
    for i in range((count + 1) // 2):
        order += [i] if count - 1 - i == i else [i, count - 1 - i]
    return order


def sweep_kernel(
    walls, harms, strip, sketch, inverse, up, down, sampled, gram,
    pieces, inverse_v, couple_v, products, partial, halo_out, halo_in,
    whole, summed, gathered, gram_out, gram_in,
    load_sem, recv_sem, send_sem, halo_send, halo_recv, gram_send, gram_recv,
):
    count, rows, width = sketch.shape
    w = lax.axis_index("wall")
    z = lax.axis_index("harm")
    prev, following = (z + harms - 1) % harms, (z + 1) % harms
    wall_bits, harm_bits = bits_of(walls), bits_of(harms)
    order = visit_order(count)

    near = min(4, harms)
    butterfly = [("wall", flip(w, b)) for b in wall_bits if b > 1]
    butterfly += [("harm", flip(z, b)) for b in harm_bits if b >= near]
    greet = [{"wall": flip(w, b)} for b in wall_bits]
    greet += [{"harm": flip(z, b)} for b in harm_bits if b >= near]
    greet += [{"harm": z - z % near + (z % near + d) % near} for d in range(1, near)]
    greet += [{"harm": prev}, {"harm": following}]
    barrier = pltpu.get_barrier_semaphore()

    loads = [
        pltpu.make_async_copy(inverse.at[h], inverse_v.at[h], load_sem.at[h]) for h in order
    ]
    loads += [
        pltpu.make_async_copy(up, couple_v.at[pl.ds(0, BAND)], load_sem.at[count]),
        pltpu.make_async_copy(down, couple_v.at[pl.ds(BAND, BAND)], load_sem.at[count + 1]),
    ]

    def block(g, h, m):
        source = w
        for b in wall_bits:
            if m & b:
                source = flip(source, b)
        return pieces.at[g, h, pl.ds(pl.multiple_of(source * rows, rows), rows)]

    own_copies = [
        pltpu.make_async_copy(sketch.at[h], block(0, h, 0), load_sem.at[count + 2 + h])
        for h in range(count)
    ]
    for copy in own_copies:
        copy.start()
    for peer in greet:
        pl.semaphore_signal(barrier, inc=1, device_id=peer, device_id_type=MESH)
    for copy in loads:
        copy.start()
    pl.semaphore_wait(barrier, len(greet))

    def hop(g, h, m, bit):
        return pltpu.make_async_remote_copy(
            src_ref=block(g, h, m), dst_ref=block(g, h, m),
            send_sem=send_sem.at[h, m + bit], recv_sem=recv_sem.at[g, h, m + bit],
            device_id={"wall": flip(w, bit)}, device_id_type=MESH,
        )

    def arrival(g, h, m):
        low = m & -m
        return pltpu.make_async_remote_copy(
            src_ref=block(g, h, m), dst_ref=block(g, h, m),
            send_sem=send_sem.at[h, m], recv_sem=recv_sem.at[g, h, m],
            device_id={"wall": flip(w, low)}, device_id_type=MESH,
        )

    def send_own(g, h):
        for bit in reversed(wall_bits):
            hop(g, h, 0, bit).start()

    def relay(g, h):
        for m in sorted(range(2, walls, 2), key=lambda m: -(m & -m)):
            arrival(g, h, m).wait_recv()
            for bit in reversed(wall_bits):
                if bit < (m & -m):
                    hop(g, h, m, bit).start()

    def finish(g, h):
        for m in range(1, walls, 2):
            arrival(g, h, m).wait_recv()

    def collect(g, h):
        relay(g, h)
        finish(g, h)

    def settle(g, h):
        for m in range(1, walls):
            arrival(g, h, m).wait_send()

    def apply_inverse(g, h):
        return jnp.dot(inverse_v[h], pieces[g, h], preferred_element_type=jnp.float32)

    def store_own(g, h, value):
        pieces[g, h, pl.ds(pl.multiple_of(w * rows, rows), rows), :] = value

    for h in order:
        own_copies[h].wait()
        send_own(0, h)

    blank = jnp.zeros((rows, width), jnp.float32)

    @pl.loop(0, 2 * BAND)
    def _(j):
        for slot in range(BAND):
            products[j, slot] = blank
            products[j, count + BAND + slot] = blank

    for i, h in enumerate(order):
        collect(0, h)
        loads[i].wait()
        state = apply_inverse(0, h).astype(jnp.bfloat16)
        settle(0, h)
        store_own(1, h, state)
        send_own(1, h)
    loads[count].wait()
    loads[count + 1].wait()

    offsets = [strip[j] + 1 for j in range(BAND)]

    def halo(s, side, i):
        return pltpu.make_async_remote_copy(
            src_ref=halo_out.at[s, side, i], dst_ref=halo_in.at[s, side, i],
            send_sem=halo_send.at[side, i], recv_sem=halo_recv.at[s, side, i],
            device_id={"harm": prev if side == 0 else following}, device_id_type=MESH,
        )

    def from_below(t):
        total = products[0, t - offsets[0] + BAND]
        for j in range(1, BAND):
            total = total + products[j, t - offsets[j] + BAND]
        shift = offsets[0] * (width // 4)
        return pltpu.roll(pltpu.roll(total, shift, 1), width - shift, 1)

    def from_above(t):
        total = products[BAND, t + offsets[0] + BAND]
        for j in range(1, BAND):
            total = total + products[BAND + j, t + offsets[j] + BAND]
        return total

    slots = []
    for i in range(BAND):
        slots.append((1, i, {count + i - o for o in range(1, BAND + 1)}))
        slots.append((0, BAND - 1 - i, {o - 1 - i for o in range(1, BAND + 1)}))
    slots = [(side, i, {h for h in need if 0 <= h < count}) for side, i, need in slots]

    for s in range(SWEEPS):
        g_state, g_rhs = 1 + 2 * s, 2 + 2 * s
        done, sent = set(), set()
        for start in range(0, count, 2):
            group, later = order[start : start + 2], order[start + 2 : start + 4]
            for h in group:
                if start == 0:
                    relay(g_state, h)
            for h in group:
                finish(g_state, h)

            def couple(j):
                state = jnp.concatenate([pieces[g_state, h] for h in group], axis=1)
                both = jnp.dot(couple_v[j], state, preferred_element_type=jnp.float32)
                for at, h in enumerate(group):
                    products[j, h + BAND] = both[:, at * width : (at + 1) * width]

            pl.loop(0, BAND, unroll=BAND)(couple)
            for h in later:
                relay(g_state, h)
            pl.loop(BAND, 2 * BAND, unroll=BAND)(couple)
            done |= set(group)
            for side, i, need in slots:
                if (side, i) not in sent and need <= done:
                    sent.add((side, i))
                    value = from_above(i - BAND) if side == 0 else from_below(count + i)
                    halo_out[s, side, i] = value.astype(jnp.bfloat16)
                    halo(s, side, i).start()
        for h in order:
            settle(g_state, h)
            own = pieces[0, h, pl.ds(pl.multiple_of(w * rows, rows), rows), :]
            partial[h] = own.astype(jnp.float32) - (from_below(h) + from_above(h))
        for h in order:
            rhs = partial[h]
            if h < BAND:
                halo(s, 1, h).wait_recv()
                rhs = rhs - halo_in[s, 1, h].astype(jnp.float32)
            if h >= count - BAND:
                i = h - count + BAND
                halo(s, 0, i).wait_recv()
                rhs = rhs - halo_in[s, 0, i].astype(jnp.float32)
            store_own(g_rhs, h, rhs.astype(jnp.bfloat16))
            send_own(g_rhs, h)
        for side in range(2):
            for i in range(BAND):
                halo(s, side, i).wait_send()
        total = jnp.zeros((width, width), jnp.float32)
        for h in order:
            collect(g_rhs, h)
            result = apply_inverse(g_rhs, h)
            settle(g_rhs, h)
            if s < SWEEPS - 1:
                store_own(g_rhs + 1, h, result.astype(jnp.bfloat16))
                send_own(g_rhs + 1, h)
            else:
                sampled[h] = result
                total = total + lax.dot_general(
                    result, result, (((0,), (0,)), ((), ())),
                    precision=lax.Precision.HIGHEST, preferred_element_type=jnp.float32,
                )

    part = width // 2
    mine, theirs = (w % 2) * part, (1 - w % 2) * part

    def swap(stage, source, target, peer):
        copy = pltpu.make_async_remote_copy(
            src_ref=source, dst_ref=target, send_sem=gram_send.at[stage],
            recv_sem=gram_recv.at[stage], device_id=peer, device_id_type=MESH,
        )
        copy.start()
        return copy

    whole[...] = total
    swap(
        0, whole.at[pl.ds(pl.multiple_of(theirs, part), part)], gram_in.at[0], {"wall": flip(w, 1)}
    ).wait()
    half = whole[pl.ds(pl.multiple_of(mine, part), part), :] + gram_in[0]
    stage = 1
    for axis, peer in butterfly:
        gram_out[stage] = half
        swap(stage, gram_out.at[stage], gram_in.at[stage], {axis: peer}).wait()
        half = half + gram_in[stage]
        stage += 1
    me = z % near
    gathered[me] = half
    copies = [
        swap(stage + d - 1, gathered.at[me], gathered.at[me], {"harm": z - me + (me + d) % near})
        for d in range(1, near)
    ]
    for copy in copies:
        copy.wait()
    half = gathered[0]
    for d in range(1, near):
        half = half + gathered[d]
    stage += near - 1
    half = half / (harms * walls * count * rows)
    place = pl.ds(pl.multiple_of(mine, part), part)
    summed[place, :] = half
    swap(stage, summed.at[place], summed.at[place], {"wall": flip(w, 1)}).wait()
    gram[...] = summed[...]


def factor_kernel(sampled, gram, basis, triangle, work, inverse_lower):
    count, rows, width = sampled.shape
    panel = 8
    row_at = lax.broadcasted_iota(jnp.int32, (width, width), 0)
    col_at = lax.broadcasted_iota(jnp.int32, (width, width), 1)
    at = lax.broadcasted_iota(jnp.int32, (panel, width), 0)
    work[...] = gram[...]
    inverse_lower[...] = jnp.where(row_at == col_at, 1.0, 0.0)

    def spread(value, i):
        return jnp.broadcast_to(value[i : i + 1, :], (panel, width))

    for low in range(0, width, panel):
        a = work[low : low + panel, :]
        x = inverse_lower[low : low + panel, :]
        columns = [
            jnp.broadcast_to(a[:, low + i : low + i + 1], (panel, width)) for i in range(panel)
        ]
        pivots = jnp.ones((panel, width), jnp.float32)
        for i in range(panel):
            pivot = spread(columns[i], i)
            pivots = jnp.where(at == i, pivot, pivots)
            factor = jnp.where(at > i, columns[i] * (1.0 / pivot), 0.0)
            for m in range(i + 1, panel):
                columns[m] = columns[m] - factor * spread(columns[m], i)
            a = a - factor * spread(a, i)
            x = x - factor * spread(x, i)
        unit = lax.rsqrt(pivots)
        a, x = a * unit, x * unit
        work[low : low + panel, :] = a
        inverse_lower[low : low + panel, :] = x
        if low + panel < width:
            change = lax.dot_general(
                a, jnp.concatenate([a, x], axis=1), (((0,), (0,)), ((), ())),
                precision=lax.Precision.HIGHEST, preferred_element_type=jnp.float32,
            )
            below = low + panel
            work[below:, :] = work[below:, :] - change[below:, :width]
            inverse_lower[below:, :] = inverse_lower[below:, :] - change[below:, width:]

    triangle[...] = jnp.where(row_at <= col_at, work[...], 0.0)
    for h in range(count):
        basis[h] = lax.dot_general(
            sampled[h], inverse_lower[...], (((1,), (1,)), ((), ())),
            precision=lax.Precision.HIGHEST, preferred_element_type=jnp.float32,
        )


def body(walls, harms, sketch, inverse_blocks, couple_up, couple_down, strip_harmonics):
    count, rows, width = sketch.shape
    size = rows * walls
    near = min(4, harms)
    stages = len(bits_of(walls)) + len(bits_of(harms // near)) + near
    gathers = 1 + 2 * SWEEPS
    vmem = pl.BlockSpec(memory_space=pltpu.VMEM)
    anywhere = pl.BlockSpec(memory_space=pl.ANY)
    sampled, gram = pl.pallas_call(
        functools.partial(sweep_kernel, walls, harms),
        out_shape=(
            jax.ShapeDtypeStruct((count, rows, width), jnp.float32),
            jax.ShapeDtypeStruct((width, width), jnp.float32),
        ),
        in_specs=[pl.BlockSpec(memory_space=pltpu.SMEM)] + [anywhere] * 4,
        out_specs=(vmem, vmem),
        scratch_shapes=[
            pltpu.VMEM((gathers, count, size, width), jnp.bfloat16),
            pltpu.VMEM((count, rows, size), jnp.bfloat16),
            pltpu.VMEM((2 * BAND, rows, size), jnp.bfloat16),
            pltpu.VMEM((2 * BAND, count + 2 * BAND, rows, width), jnp.float32),
            pltpu.VMEM((count, rows, width), jnp.float32),
            pltpu.VMEM((SWEEPS, 2, BAND, rows, width), jnp.bfloat16),
            pltpu.VMEM((SWEEPS, 2, BAND, rows, width), jnp.bfloat16),
            pltpu.VMEM((width, width), jnp.float32),
            pltpu.VMEM((width, width), jnp.float32),
            pltpu.VMEM((near, width // 2, width), jnp.float32),
            pltpu.VMEM((stages, width // 2, width), jnp.float32),
            pltpu.VMEM((stages, width // 2, width), jnp.float32),
            pltpu.SemaphoreType.DMA((2 * count + 2,)),
            pltpu.SemaphoreType.DMA((gathers, count, walls)),
            pltpu.SemaphoreType.DMA((count, walls)),
            pltpu.SemaphoreType.DMA((2, BAND)),
            pltpu.SemaphoreType.DMA((SWEEPS, 2, BAND)),
            pltpu.SemaphoreType.DMA((stages,)),
            pltpu.SemaphoreType.DMA((stages,)),
        ],
        compiler_params=pltpu.CompilerParams(
            collective_id=0, has_side_effects=True, vmem_limit_bytes=67043328
        ),
        name="sweeps",
    )(strip_harmonics, sketch, inverse_blocks, couple_up, couple_down)
    return pl.pallas_call(
        factor_kernel,
        out_shape=(
            jax.ShapeDtypeStruct((count, rows, width), jnp.float32),
            jax.ShapeDtypeStruct((width, width), jnp.float32),
        ),
        in_specs=[vmem, vmem],
        out_specs=(vmem, vmem),
        scratch_shapes=[pltpu.VMEM((width, width), jnp.float32)] * 2,
        name="factor",
    )(sampled, gram)


def solution(mesh):
    return jax.shard_map(
        functools.partial(body, mesh.shape["wall"], mesh.shape["harm"]),
        mesh=mesh,
        in_specs=(
            P(("freq", "harm"), "wall", None),
            P(("freq", "harm"), "wall", None),
            P("freq", "wall", None),
            P("freq", "wall", None),
            P("freq"),
        ),
        out_specs=(P(("freq", "harm"), "wall", None), P("freq", None)),
        check_vma=False,
    )
```

```python
import functools

import jax
import jax.numpy as jnp
from jax import lax
from jax.experimental import pallas as pl
from jax.experimental.pallas import tpu as pltpu
from jax.sharding import PartitionSpec as P

BAND = 4
SWEEPS = 3
MESH = pl.DeviceIdType.MESH


def flip(index, bit):
    return index + bit - 2 * bit * (lax.div(index, bit) % 2)


def bits_of(count):
    return [1 << b for b in range(count.bit_length() - 1)]


def plan(count):
    last = count - 1
    steps = []
    for s in range(-1, SWEEPS + 1):
        steps += [("couple", s, 0), ("relay rhs", s - 1, last)]
        steps += [("relay state", s, 1), ("solve", s - 1, last), ("couple", s, 1)]
        for c in range(2, count):
            steps += [("relay state", s, c), ("couple", s, c), ("correct", s, c - 2)]
        steps += [("relay rhs", s, 0), ("solve", s, 0)]
        for c in range(1, last):
            steps += [("correct", s, c + 1), ("relay rhs", s, c)]
            if c == last - 1:
                steps += [("relay state", s + 1, 0)]
            steps += [("solve", s, c)]
    def holds(step, s, c):
        if step == "relay state":
            return 0 <= s < SWEEPS
        return (-1 if step in ("relay rhs", "solve") else 0) <= s < SWEEPS
    return [entry for entry in steps if holds(*entry)]


def sweep_kernel(
    walls, harms, strip, sketch, inverse, up, down, sampled, gram,
    sketch_v, pieces, inverse_v, couple_v, partial, halo_out, halo_in,
    whole, summed, gathered, gram_out, gram_in,
    load_sem, recv_sem, send_sem, halo_send, halo_recv, gram_send, gram_recv,
):
    count, rows, width = sketch.shape
    lanes = width // count
    w = lax.axis_index("wall")
    z = lax.axis_index("harm")
    prev, following = (z + harms - 1) % harms, (z + 1) % harms
    wall_bits, harm_bits = bits_of(walls), bits_of(harms)
    lane = lax.broadcasted_iota(jnp.int32, (rows, width), 1)

    near = min(4, harms)
    butterfly = [("wall", flip(w, b)) for b in wall_bits if b > 1]
    butterfly += [("harm", flip(z, b)) for b in harm_bits if b >= near]
    greet = [{"wall": flip(w, b)} for b in wall_bits]
    greet += [{"harm": flip(z, b)} for b in harm_bits if b >= near]
    greet += [{"harm": z - z % near + (z % near + d) % near} for d in range(1, near)]
    greet += [{"harm": prev}, {"harm": following}]
    barrier = pltpu.get_barrier_semaphore()

    own_copy = pltpu.make_async_copy(sketch, sketch_v, load_sem.at[count + 2])
    own_copy.start()
    for peer in greet:
        pl.semaphore_signal(barrier, inc=1, device_id=peer, device_id_type=MESH)
    inverse_loads = [
        pltpu.make_async_copy(inverse.at[h], inverse_v.at[h], load_sem.at[h]) for h in range(count)
    ]
    couple_loads = [
        pltpu.make_async_copy(up, couple_v.at[pl.ds(0, BAND)], load_sem.at[count]),
        pltpu.make_async_copy(down, couple_v.at[pl.ds(BAND, BAND)], load_sem.at[count + 1]),
    ]
    for copy in inverse_loads + couple_loads:
        copy.start()

    def block(g, c, m):
        source = w
        for b in wall_bits:
            if m & b:
                source = flip(source, b)
        return pieces.at[g, c, pl.ds(pl.multiple_of(source * rows, rows), rows)]

    def hop(g, c, m, bit):
        return pltpu.make_async_remote_copy(
            src_ref=block(g, c, m), dst_ref=block(g, c, m),
            send_sem=send_sem.at[g, c, m + bit], recv_sem=recv_sem.at[g, c, m + bit],
            device_id={"wall": flip(w, bit)}, device_id_type=MESH,
        )

    def arrival(g, c, m):
        low = m & -m
        return pltpu.make_async_remote_copy(
            src_ref=block(g, c, m), dst_ref=block(g, c, m),
            send_sem=send_sem.at[g, c, m], recv_sem=recv_sem.at[g, c, m],
            device_id={"wall": flip(w, low)}, device_id_type=MESH,
        )

    def send_own(g, c):
        for bit in reversed(wall_bits):
            hop(g, c, 0, bit).start()

    def relay(g, c):
        for m in sorted(range(2, walls, 2), key=lambda m: -(m & -m)):
            arrival(g, c, m).wait_recv()
            for bit in reversed(wall_bits):
                if bit < (m & -m):
                    hop(g, c, m, bit).start()

    def finish(g, c):
        for m in range(1, walls, 2):
            arrival(g, c, m).wait_recv()

    def own(c):
        return pl.ds(pl.multiple_of(w * rows, rows), rows)

    def halo(s, side, c):
        return pltpu.make_async_remote_copy(
            src_ref=halo_out.at[s, side, c], dst_ref=halo_in.at[s, side, c],
            send_sem=halo_send.at[s, side, c], recv_sem=halo_recv.at[s, side, c],
            device_id={"harm": prev if side == 0 else following}, device_id_type=MESH,
        )

    def start(c):
        tile = None
        for h in range(count):
            turn = (h - c) % count * lanes
            source = sketch_v[h].astype(jnp.float32)
            source = source if turn == 0 else pltpu.roll(source, turn, 1)
            tile = source if tile is None else jnp.where(lane < h * lanes, tile, source)
        pieces[0, c, own(c), :] = tile.astype(jnp.bfloat16)
        send_own(0, c)

    shifts = [(strip[j] + 1) * lanes for j in range(BAND)]

    def couple(s, c):
        g = 2 * s + 1
        finish(g, c)
        local = pieces[0, c, own(c), :].astype(jnp.float32)
        away = jnp.zeros((rows, width), jnp.float32)
        for j in range(BAND):
            product = jnp.dot(couple_v[j], pieces[g, c], preferred_element_type=jnp.float32)
            product = pltpu.roll(product, lax.rem(shifts[j], width), 1)
            stays = lane >= shifts[j]
            local = local - jnp.where(stays, product, 0.0)
            away = away + jnp.where(stays, 0.0, product)
        halo_out[s, 1, c] = away.astype(jnp.bfloat16)
        halo(s, 1, c).start()
        away = jnp.zeros((rows, width), jnp.float32)
        for j in range(BAND):
            product = jnp.dot(couple_v[BAND + j], pieces[g, c], preferred_element_type=jnp.float32)
            product = pltpu.roll(product, width - shifts[j], 1)
            stays = lane < width - shifts[j]
            local = local - jnp.where(stays, product, 0.0)
            away = away + jnp.where(stays, 0.0, product)
        halo_out[s, 0, c] = away.astype(jnp.bfloat16)
        halo(s, 0, c).start()
        partial[c] = local

    def correct(s, c):
        rhs = partial[c]
        for side in (1, 0):
            halo(s, side, c).wait_recv()
            rhs = rhs - halo_in[s, side, c].astype(jnp.float32)
        pieces[2 * s + 2, c, own(c), :] = rhs.astype(jnp.bfloat16)
        send_own(2 * s + 2, c)

    def solve(s, c):
        g = 2 * s + 2
        finish(g, c)
        result = None
        for h in range(count):
            product = jnp.dot(inverse_v[h], pieces[g, c], preferred_element_type=jnp.float32)
            result = product if result is None else jnp.where(lane < h * lanes, result, product)
        if s < SWEEPS - 1:
            pieces[g + 1, c, own(c), :] = result.astype(jnp.bfloat16)
            send_own(g + 1, c)
        else:
            partial[c] = result

    pl.semaphore_wait(barrier, len(greet))
    own_copy.wait()
    for c in range(count):
        start(c)
    ready = set()
    for step, s, c in plan(count):
        if step == "solve" and "inverse" not in ready:
            ready.add("inverse")
            for copy in inverse_loads:
                copy.wait()
        if step == "couple" and "couple" not in ready:
            ready.add("couple")
            for copy in couple_loads:
                copy.wait()
        if step == "relay rhs":
            relay(2 * s + 2, c)
        elif step == "relay state":
            relay(2 * s + 1, c)
        else:
            {"solve": solve, "couple": couple, "correct": correct}[step](s, c)

    total = jnp.zeros((width, width), jnp.float32)
    for h in range(count):
        tile = None
        for c in range(count):
            turn = (c - h) % count * lanes
            source = partial[c] if turn == 0 else pltpu.roll(partial[c], turn, 1)
            tile = source if tile is None else jnp.where(lane < c * lanes, tile, source)
        sampled[h] = tile
        total = total + lax.dot_general(
            tile, tile, (((0,), (0,)), ((), ())),
            precision=lax.Precision.HIGHEST, preferred_element_type=jnp.float32,
        )

    part = width // 2
    mine, theirs = (w % 2) * part, (1 - w % 2) * part

    def swap(stage, source, target, peer):
        copy = pltpu.make_async_remote_copy(
            src_ref=source, dst_ref=target, send_sem=gram_send.at[stage],
            recv_sem=gram_recv.at[stage], device_id=peer, device_id_type=MESH,
        )
        copy.start()
        return copy

    whole[...] = total
    swap(
        0, whole.at[pl.ds(pl.multiple_of(theirs, part), part)], gram_in.at[0], {"wall": flip(w, 1)}
    ).wait()
    half = whole[pl.ds(pl.multiple_of(mine, part), part), :] + gram_in[0]
    stage = 1
    for axis, peer in butterfly:
        gram_out[stage] = half
        swap(stage, gram_out.at[stage], gram_in.at[stage], {axis: peer}).wait()
        half = half + gram_in[stage]
        stage += 1
    me = z % near
    gathered[me] = half
    copies = [
        swap(stage + d - 1, gathered.at[me], gathered.at[me], {"harm": z - me + (me + d) % near})
        for d in range(1, near)
    ]
    for copy in copies:
        copy.wait()
    half = gathered[0]
    for d in range(1, near):
        half = half + gathered[d]
    stage += near - 1
    half = half / (harms * walls * count * rows)
    place = pl.ds(pl.multiple_of(mine, part), part)
    summed[place, :] = half
    swap(stage, summed.at[place], summed.at[place], {"wall": flip(w, 1)}).wait()
    gram[...] = summed[...]
    for c in range(count):
        for g in range(2 * SWEEPS + 1):
            for m in range(1, walls):
                arrival(g, c, m).wait_send()
        for s in range(SWEEPS):
            for side in range(2):
                halo(s, side, c).wait_send()


def factor_kernel(sampled, gram, basis, triangle, work, inverse_lower):
    count, rows, width = sampled.shape
    panel = 8
    row_at = lax.broadcasted_iota(jnp.int32, (width, width), 0)
    col_at = lax.broadcasted_iota(jnp.int32, (width, width), 1)
    at = lax.broadcasted_iota(jnp.int32, (panel, width), 0)
    work[...] = gram[...]
    inverse_lower[...] = jnp.where(row_at == col_at, 1.0, 0.0)

    def spread(value, i):
        return jnp.broadcast_to(value[i : i + 1, :], (panel, width))

    for low in range(0, width, panel):
        a = work[low : low + panel, :]
        x = inverse_lower[low : low + panel, :]
        columns = [
            jnp.broadcast_to(a[:, low + i : low + i + 1], (panel, width)) for i in range(panel)
        ]
        pivots = jnp.ones((panel, width), jnp.float32)
        for i in range(panel):
            pivot = spread(columns[i], i)
            pivots = jnp.where(at == i, pivot, pivots)
            factor = jnp.where(at > i, columns[i] * (1.0 / pivot), 0.0)
            for m in range(i + 1, panel):
                columns[m] = columns[m] - factor * spread(columns[m], i)
            a = a - factor * spread(a, i)
            x = x - factor * spread(x, i)
        unit = lax.rsqrt(pivots)
        a, x = a * unit, x * unit
        work[low : low + panel, :] = a
        inverse_lower[low : low + panel, :] = x
        if low + panel < width:
            change = lax.dot_general(
                a, jnp.concatenate([a, x], axis=1), (((0,), (0,)), ((), ())),
                precision=lax.Precision.HIGHEST, preferred_element_type=jnp.float32,
            )
            below = low + panel
            work[below:, :] = work[below:, :] - change[below:, :width]
            inverse_lower[below:, :] = inverse_lower[below:, :] - change[below:, width:]

    triangle[...] = jnp.where(row_at <= col_at, work[...], 0.0)
    for h in range(count):
        basis[h] = lax.dot_general(
            sampled[h], inverse_lower[...], (((1,), (1,)), ((), ())),
            precision=lax.Precision.HIGHEST, preferred_element_type=jnp.float32,
        )


def body(walls, harms, sketch, inverse_blocks, couple_up, couple_down, strip_harmonics):
    count, rows, width = sketch.shape
    size = rows * walls
    near = min(4, harms)
    stages = len(bits_of(walls)) + len(bits_of(harms // near)) + near
    gathers = 1 + 2 * SWEEPS
    vmem = pl.BlockSpec(memory_space=pltpu.VMEM)
    anywhere = pl.BlockSpec(memory_space=pl.ANY)
    sampled, gram = pl.pallas_call(
        functools.partial(sweep_kernel, walls, harms),
        out_shape=(
            jax.ShapeDtypeStruct((count, rows, width), jnp.float32),
            jax.ShapeDtypeStruct((width, width), jnp.float32),
        ),
        in_specs=[pl.BlockSpec(memory_space=pltpu.SMEM)] + [anywhere] * 4,
        out_specs=(vmem, vmem),
        scratch_shapes=[
            pltpu.VMEM((count, rows, width), jnp.bfloat16),
            pltpu.VMEM((gathers, count, size, width), jnp.bfloat16),
            pltpu.VMEM((count, rows, size), jnp.bfloat16),
            pltpu.VMEM((2 * BAND, rows, size), jnp.bfloat16),
            pltpu.VMEM((count, rows, width), jnp.float32),
            pltpu.VMEM((SWEEPS, 2, count, rows, width), jnp.bfloat16),
            pltpu.VMEM((SWEEPS, 2, count, rows, width), jnp.bfloat16),
            pltpu.VMEM((width, width), jnp.float32),
            pltpu.VMEM((width, width), jnp.float32),
            pltpu.VMEM((near, width // 2, width), jnp.float32),
            pltpu.VMEM((stages, width // 2, width), jnp.float32),
            pltpu.VMEM((stages, width // 2, width), jnp.float32),
            pltpu.SemaphoreType.DMA((count + 3,)),
            pltpu.SemaphoreType.DMA((gathers, count, walls)),
            pltpu.SemaphoreType.DMA((gathers, count, walls)),
            pltpu.SemaphoreType.DMA((SWEEPS, 2, count)),
            pltpu.SemaphoreType.DMA((SWEEPS, 2, count)),
            pltpu.SemaphoreType.DMA((stages,)),
            pltpu.SemaphoreType.DMA((stages,)),
        ],
        compiler_params=pltpu.CompilerParams(
            collective_id=0, has_side_effects=True, vmem_limit_bytes=67043328
        ),
        name="sweeps",
    )(strip_harmonics, sketch, inverse_blocks, couple_up, couple_down)
    return pl.pallas_call(
        factor_kernel,
        out_shape=(
            jax.ShapeDtypeStruct((count, rows, width), jnp.float32),
            jax.ShapeDtypeStruct((width, width), jnp.float32),
        ),
        in_specs=[vmem, vmem],
        out_specs=(vmem, vmem),
        scratch_shapes=[pltpu.VMEM((width, width), jnp.float32)] * 2,
        name="factor",
    )(sampled, gram)


def solution(mesh):
    return jax.shard_map(
        functools.partial(body, mesh.shape["wall"], mesh.shape["harm"]),
        mesh=mesh,
        in_specs=(
            P(("freq", "harm"), "wall", None),
            P(("freq", "harm"), "wall", None),
            P("freq", "wall", None),
            P("freq", "wall", None),
            P("freq"),
        ),
        out_specs=(P(("freq", "harm"), "wall", None), P("freq", None)),
        check_vma=False,
    )
```

```python
import functools

import jax
import jax.numpy as jnp
from jax import lax
from jax.experimental import pallas as pl
from jax.experimental.pallas import tpu as pltpu
from jax.sharding import PartitionSpec as P

BAND = 4
SWEEPS = 3
MESH = pl.DeviceIdType.MESH


def flip(index, bit):
    return index + bit - 2 * bit * (lax.div(index, bit) % 2)


def bits_of(count):
    return [1 << b for b in range(count.bit_length() - 1)]


STEPS = (
    ("couple near", 0, 0), ("couple mid", 0, 0), ("solve mid", 2, 1), ("solve near", 3, 1),
    ("couple far", 0, 0), ("solve far", 2, 1), ("couple near", 1, 0), ("couple mid", 1, 0),
    ("solve mid", 3, 1), ("couple far", 1, 0), ("solve far", 3, 1), ("couple near", 2, 0),
    ("couple mid", 2, 0), ("couple near", 3, 0), ("couple far", 2, 0), ("correct", 0, 0),
    ("couple mid", 3, 0), ("couple far", 3, 0), ("correct", 1, 0), ("solve near", 0, 0),
    ("solve mid", 0, 0), ("solve near", 1, 0), ("solve far", 0, 0), ("correct", 2, 0),
    ("solve mid", 1, 0), ("solve near", 2, 0), ("solve far", 1, 0), ("correct", 3, 0),
)


def steps_of(count):
    if count == 4:
        return STEPS
    names = ("couple near", "couple mid", "couple far", "correct", "solve near", "solve mid", "solve far")
    return tuple((name, c, 0) for name in names for c in range(count))


def sweep_kernel(
    walls, harms, strip, sketch, inverse, up, down, sampled, gram,
    sketch_v, pieces, inverse_v, couple_v, solved, local, away, halo_out, halo_in,
    whole, summed, gathered, gram_out, gram_in,
    load_sem, recv_sem, send_sem, halo_send, halo_recv, gram_send, gram_recv,
):
    count, rows, width = sketch.shape
    lanes = width // count
    w = lax.axis_index("wall")
    z = lax.axis_index("harm")
    prev, following = (z + harms - 1) % harms, (z + 1) % harms
    wall_bits, harm_bits = bits_of(walls), bits_of(harms)
    lane = lax.broadcasted_iota(jnp.int32, (rows, width), 1)

    near = min(4, harms)
    butterfly = [("wall", flip(w, b)) for b in wall_bits if b > 1]
    butterfly += [("harm", flip(z, b)) for b in harm_bits if b >= near]
    greet = [{"wall": flip(w, b)} for b in wall_bits]
    greet += [{"harm": flip(z, b)} for b in harm_bits if b >= near]
    greet += [{"harm": z - z % near + (z % near + d) % near} for d in range(1, near)]
    greet += [{"harm": prev}, {"harm": following}]
    barrier = pltpu.get_barrier_semaphore()

    own_copy = pltpu.make_async_copy(sketch, sketch_v, load_sem.at[0])
    own_copy.start()
    for peer in greet:
        pl.semaphore_signal(barrier, inc=1, device_id=peer, device_id_type=MESH)

    inverse_loads, couple_loads = [], []
    for m in range(walls):
        source = w
        for b in wall_bits:
            if m & b:
                source = flip(source, b)
        there = pl.ds(pl.multiple_of(source * rows, rows), rows)
        here = pl.ds(m * rows, rows)
        inverse_loads.append(pltpu.make_async_copy(
            inverse.at[:, :, there], inverse_v.at[:, :, here], load_sem.at[1 + m]
        ))
        for at, matrix in enumerate((up, down)):
            couple_loads.append(pltpu.make_async_copy(
                matrix.at[:, :, there], couple_v.at[at, :, :, here],
                load_sem.at[1 + walls * (1 + at) + m],
            ))
    for copy in inverse_loads + couple_loads:
        copy.start()

    def hop(g, c, m, bit):
        return pltpu.make_async_remote_copy(
            src_ref=pieces.at[g, c, m], dst_ref=pieces.at[g, c, m + bit],
            send_sem=send_sem.at[g, c, m + bit], recv_sem=recv_sem.at[g, c, m + bit],
            device_id={"wall": flip(w, bit)}, device_id_type=MESH,
        )

    def arrival(g, c, m):
        low = m & -m
        return hop(g, c, m - low, low)

    def send_own(g, c):
        for bit in reversed(wall_bits):
            hop(g, c, 0, bit).start()

    relayed = sorted(range(2, walls, 2), key=lambda m: -(m & -m))
    spans = {
        "near": [(0, min(2, walls))],
        "mid": [(m, m + 1) for m in range(2, walls, 2)],
        "far": [(m, m + 1) for m in range(3, walls, 2)],
    }

    def collect(part, g, c):
        if part == "near":
            if walls > 1:
                arrival(g, c, 1).wait_recv()
        elif part == "mid":
            for m in relayed:
                arrival(g, c, m).wait_recv()
                for bit in reversed(wall_bits):
                    if bit < (m & -m):
                        hop(g, c, m, bit).start()
        else:
            for m in range(3, walls, 2):
                arrival(g, c, m).wait_recv()

    def times(matrix, g, c, low, high):
        piece = pieces[g, c, low:high].reshape((high - low) * rows, width)
        return jnp.dot(
            matrix[:, low * rows : high * rows], piece, preferred_element_type=jnp.float32
        )

    def halo(s, side, c):
        return pltpu.make_async_remote_copy(
            src_ref=halo_out.at[s, side, c], dst_ref=halo_in.at[s, side, c],
            send_sem=halo_send.at[s, side, c], recv_sem=halo_recv.at[s, side, c],
            device_id={"harm": prev if side == 0 else following}, device_id_type=MESH,
        )

    def start(c):
        tile = None
        for h in range(count):
            turn = (h - c) % count * lanes
            source = sketch_v[h].astype(jnp.float32)
            source = source if turn == 0 else pltpu.roll(source, turn, 1)
            tile = source if tile is None else jnp.where(lane < h * lanes, tile, source)
        pieces[0, c, 0] = tile.astype(jnp.bfloat16)
        send_own(0, c)

    shifts = [(strip[j] + 1) * lanes for j in range(BAND)]

    def couple(part, s, c):
        g = 2 * s + 1
        collect(part, g, c)
        if part == "near":
            inner = pieces[0, c, 0].astype(jnp.float32)
        else:
            inner = local[c]
        for side in (1, 0):
            outer = jnp.zeros((rows, width), jnp.float32) if part == "near" else away[side, c]
            for j in range(BAND):
                if side == 1:
                    turn, stays = lax.rem(shifts[j], width), lane >= shifts[j]
                else:
                    turn, stays = width - shifts[j], lane < width - shifts[j]
                for low, high in spans[part]:
                    product = times(couple_v.at[1 - side, j], g, c, low, high)
                    product = pltpu.roll(product, turn, 1)
                    inner = inner - jnp.where(stays, product, 0.0)
                    outer = outer + jnp.where(stays, 0.0, product)
            if part == "far":
                halo_out[s, side, c] = outer.astype(jnp.bfloat16)
                halo(s, side, c).start()
            else:
                away[side, c] = outer
        local[c] = inner

    def correct(s, c):
        rhs = local[c]
        for side in (1, 0):
            halo(s, side, c).wait_recv()
            rhs = rhs - halo_in[s, side, c].astype(jnp.float32)
        pieces[2 * s + 2, c, 0] = rhs.astype(jnp.bfloat16)
        send_own(2 * s + 2, c)

    def solve(part, s, c):
        g = 2 * s + 2
        collect(part, g, c)
        total = None
        for low, high in spans[part]:
            result = None
            for h in range(count):
                product = times(inverse_v.at[h], g, c, low, high)
                result = product if result is None else jnp.where(lane < h * lanes, result, product)
            total = result if total is None else total + result
        if part != "near":
            total = solved[c] + total
        if part == "far":
            @pl.when(s < SWEEPS - 1)
            def _():
                pieces[g + 1, c, 0] = total.astype(jnp.bfloat16)
                send_own(g + 1, c)
        solved[c] = total

    def take(steps, s):
        for name, c, lag in steps:
            kind, _, part = name.partition(" ")
            if kind == "couple":
                couple(part, s, c)
            elif kind == "correct":
                correct(s, c)
            else:
                solve(part, s - lag, c)

    pl.semaphore_wait(barrier, len(greet))
    own_copy.wait()
    for c in range(count):
        start(c)
    for copy in inverse_loads:
        copy.wait()
    steps = steps_of(count)
    solves = [step for step in steps if step[0].startswith("solve")]
    take([step for step in solves if step[2] == 0], -1)
    for copy in couple_loads:
        copy.wait()
    pl.loop(0, SWEEPS)(lambda s: take(steps, s))
    take([step for step in solves if step[2] == 1], SWEEPS)

    total = jnp.zeros((width, width), jnp.float32)
    for h in range(count):
        tile = None
        for c in range(count):
            turn = (c - h) % count * lanes
            source = solved[c] if turn == 0 else pltpu.roll(solved[c], turn, 1)
            tile = source if tile is None else jnp.where(lane < c * lanes, tile, source)
        sampled[h] = tile
        total = total + lax.dot_general(
            tile, tile, (((0,), (0,)), ((), ())),
            precision=lax.Precision.HIGHEST, preferred_element_type=jnp.float32,
        )

    part = width // 2
    mine, theirs = (w % 2) * part, (1 - w % 2) * part

    def swap(stage, source, target, peer):
        copy = pltpu.make_async_remote_copy(
            src_ref=source, dst_ref=target, send_sem=gram_send.at[stage],
            recv_sem=gram_recv.at[stage], device_id=peer, device_id_type=MESH,
        )
        copy.start()
        return copy

    whole[...] = total
    swap(
        0, whole.at[pl.ds(pl.multiple_of(theirs, part), part)], gram_in.at[0], {"wall": flip(w, 1)}
    ).wait()
    half = whole[pl.ds(pl.multiple_of(mine, part), part), :] + gram_in[0]
    stage = 1
    for axis, peer in butterfly:
        gram_out[stage] = half
        swap(stage, gram_out.at[stage], gram_in.at[stage], {axis: peer}).wait()
        half = half + gram_in[stage]
        stage += 1
    me = z % near
    gathered[me] = half
    copies = [
        swap(stage + d - 1, gathered.at[me], gathered.at[me], {"harm": z - me + (me + d) % near})
        for d in range(1, near)
    ]
    for copy in copies:
        copy.wait()
    half = gathered[0]
    for d in range(1, near):
        half = half + gathered[d]
    stage += near - 1
    half = half / (harms * walls * count * rows)
    place = pl.ds(pl.multiple_of(mine, part), part)
    summed[place, :] = half
    swap(stage, summed.at[place], summed.at[place], {"wall": flip(w, 1)}).wait()
    gram[...] = summed[...]

    @pl.loop(0, 2 * SWEEPS + 1)
    def _(g):
        for c in range(count):
            for m in range(1, walls):
                arrival(g, c, m).wait_send()

    @pl.loop(0, SWEEPS)
    def _(s):
        for c in range(count):
            for side in range(2):
                halo(s, side, c).wait_send()


def factor_kernel(sampled, gram, basis, triangle, work, inverse_lower):
    count, rows, width = sampled.shape
    panel = 8
    row_at = lax.broadcasted_iota(jnp.int32, (width, width), 0)
    col_at = lax.broadcasted_iota(jnp.int32, (width, width), 1)
    at = lax.broadcasted_iota(jnp.int32, (panel, width), 0)
    work[...] = gram[...]
    inverse_lower[...] = jnp.where(row_at == col_at, 1.0, 0.0)

    def spread(value, i):
        return jnp.broadcast_to(value[i : i + 1, :], (panel, width))

    for low in range(0, width, panel):
        a = work[low : low + panel, :]
        x = inverse_lower[low : low + panel, :]
        columns = [
            jnp.broadcast_to(a[:, low + i : low + i + 1], (panel, width)) for i in range(panel)
        ]
        pivots = jnp.ones((panel, width), jnp.float32)
        for i in range(panel):
            pivot = spread(columns[i], i)
            pivots = jnp.where(at == i, pivot, pivots)
            factor = jnp.where(at > i, columns[i] * (1.0 / pivot), 0.0)
            for m in range(i + 1, panel):
                columns[m] = columns[m] - factor * spread(columns[m], i)
            a = a - factor * spread(a, i)
            x = x - factor * spread(x, i)
        unit = lax.rsqrt(pivots)
        a, x = a * unit, x * unit
        work[low : low + panel, :] = a
        inverse_lower[low : low + panel, :] = x
        if low + panel < width:
            change = lax.dot_general(
                a, jnp.concatenate([a, x], axis=1), (((0,), (0,)), ((), ())),
                precision=lax.Precision.HIGHEST, preferred_element_type=jnp.float32,
            )
            below = low + panel
            work[below:, :] = work[below:, :] - change[below:, :width]
            inverse_lower[below:, :] = inverse_lower[below:, :] - change[below:, width:]

    triangle[...] = jnp.where(row_at <= col_at, work[...], 0.0)
    for h in range(count):
        basis[h] = lax.dot_general(
            sampled[h], inverse_lower[...], (((1,), (1,)), ((), ())),
            precision=lax.Precision.HIGHEST, preferred_element_type=jnp.float32,
        )


def body(walls, harms, sketch, inverse_blocks, couple_up, couple_down, strip_harmonics):
    count, rows, width = sketch.shape
    size = rows * walls
    near = min(4, harms)
    stages = len(bits_of(walls)) + len(bits_of(harms // near)) + near
    gathers = 1 + 2 * SWEEPS
    vmem = pl.BlockSpec(memory_space=pltpu.VMEM)
    anywhere = pl.BlockSpec(memory_space=pl.ANY)
    sampled, gram = pl.pallas_call(
        functools.partial(sweep_kernel, walls, harms),
        out_shape=(
            jax.ShapeDtypeStruct((count, rows, width), jnp.float32),
            jax.ShapeDtypeStruct((width, width), jnp.float32),
        ),
        in_specs=[pl.BlockSpec(memory_space=pltpu.SMEM)] + [anywhere] * 4,
        out_specs=(vmem, vmem),
        scratch_shapes=[
            pltpu.VMEM((count, rows, width), jnp.bfloat16),
            pltpu.VMEM((gathers, count, walls, rows, width), jnp.bfloat16),
            pltpu.VMEM((count, rows, size), jnp.bfloat16),
            pltpu.VMEM((2, BAND, rows, size), jnp.bfloat16),
            pltpu.VMEM((count, rows, width), jnp.float32),
            pltpu.VMEM((count, rows, width), jnp.float32),
            pltpu.VMEM((2, count, rows, width), jnp.float32),
            pltpu.VMEM((SWEEPS, 2, count, rows, width), jnp.bfloat16),
            pltpu.VMEM((SWEEPS, 2, count, rows, width), jnp.bfloat16),
            pltpu.VMEM((width, width), jnp.float32),
            pltpu.VMEM((width, width), jnp.float32),
            pltpu.VMEM((near, width // 2, width), jnp.float32),
            pltpu.VMEM((stages, width // 2, width), jnp.float32),
            pltpu.VMEM((stages, width // 2, width), jnp.float32),
            pltpu.SemaphoreType.DMA((1 + 3 * walls,)),
            pltpu.SemaphoreType.DMA((gathers, count, walls)),
            pltpu.SemaphoreType.DMA((gathers, count, walls)),
            pltpu.SemaphoreType.DMA((SWEEPS, 2, count)),
            pltpu.SemaphoreType.DMA((SWEEPS, 2, count)),
            pltpu.SemaphoreType.DMA((stages,)),
            pltpu.SemaphoreType.DMA((stages,)),
        ],
        compiler_params=pltpu.CompilerParams(
            collective_id=0, has_side_effects=True, vmem_limit_bytes=67043328
        ),
        name="sweeps",
    )(strip_harmonics, sketch, inverse_blocks, couple_up, couple_down)
    return pl.pallas_call(
        factor_kernel,
        out_shape=(
            jax.ShapeDtypeStruct((count, rows, width), jnp.float32),
            jax.ShapeDtypeStruct((width, width), jnp.float32),
        ),
        in_specs=[vmem, vmem],
        out_specs=(vmem, vmem),
        scratch_shapes=[pltpu.VMEM((width, width), jnp.float32)] * 2,
        name="factor",
    )(sampled, gram)


def solution(mesh):
    return jax.shard_map(
        functools.partial(body, mesh.shape["wall"], mesh.shape["harm"]),
        mesh=mesh,
        in_specs=(
            P(("freq", "harm"), "wall", None),
            P(("freq", "harm"), "wall", None),
            P("freq", "wall", None),
            P("freq", "wall", None),
            P("freq"),
        ),
        out_specs=(P(("freq", "harm"), "wall", None), P("freq", None)),
        check_vma=False,
    )
```

```python
import functools

import jax
import jax.numpy as jnp
from jax import lax
from jax.experimental import pallas as pl
from jax.experimental.pallas import tpu as pltpu
from jax.sharding import PartitionSpec as P

BAND = 4
SWEEPS = 3
MESH = pl.DeviceIdType.MESH


def flip(index, bit):
    return index + bit - 2 * bit * (lax.div(index, bit) % 2)


def bits_of(count):
    return [1 << b for b in range(count.bit_length() - 1)]


STEPS = (
    ("couple near", 0, 0), ("couple mid", 0, 0), ("solve mid", 2, 1), ("solve near", 3, 1),
    ("couple far", 0, 0), ("solve far", 2, 1), ("couple near", 1, 0), ("couple mid", 1, 0),
    ("solve mid", 3, 1), ("couple far", 1, 0), ("solve far", 3, 1), ("couple near", 2, 0),
    ("couple mid", 2, 0), ("couple near", 3, 0), ("couple far", 2, 0), ("correct", 0, 0),
    ("couple mid", 3, 0), ("couple far", 3, 0), ("correct", 1, 0), ("solve near", 0, 0),
    ("solve mid", 0, 0), ("solve near", 1, 0), ("solve far", 0, 0), ("correct", 2, 0),
    ("solve mid", 1, 0), ("solve near", 2, 0), ("solve far", 1, 0), ("correct", 3, 0),
)


def steps_of(count):
    if count == 4:
        return STEPS
    names = ("couple near", "couple mid", "couple far", "correct", "solve near", "solve mid", "solve far")
    return tuple((name, c, 0) for name in names for c in range(count))


def sweep_kernel(
    walls, harms, strip_in, sketch, inverse, up, down, sampled, gram,
    strip, sampled_v, sketch_v, pieces, inverse_v, couple_v, solved, local, away, halo_out, halo_in,
    whole, summed, gathered, gram_out, gram_in,
    load_sem, recv_sem, send_sem, halo_send, halo_recv, gram_send, gram_recv,
):
    count, rows, width = sketch.shape
    lanes = width // count
    w = lax.axis_index("wall")
    z = lax.axis_index("harm")
    prev, following = (z + harms - 1) % harms, (z + 1) % harms
    wall_bits, harm_bits = bits_of(walls), bits_of(harms)
    lane = lax.broadcasted_iota(jnp.int32, (rows, width), 1)

    near = min(4, harms)
    butterfly = [("wall", flip(w, b)) for b in wall_bits if b > 1]
    butterfly += [("harm", flip(z, b)) for b in harm_bits if b >= near]
    greet = [{"wall": flip(w, b)} for b in wall_bits]
    greet += [{"harm": flip(z, b)} for b in harm_bits if b >= near]
    greet += [{"harm": z - z % near + (z % near + d) % near} for d in range(1, near)]
    greet += [{"harm": prev}, {"harm": following}]
    barrier = pltpu.get_barrier_semaphore()

    own_copy = pltpu.make_async_copy(sketch, sketch_v, load_sem.at[0])
    own_copy.start()
    strip_copy = pltpu.make_async_copy(strip_in, strip, load_sem.at[1 + 3 * walls])
    strip_copy.start()
    for peer in greet:
        pl.semaphore_signal(barrier, inc=1, device_id=peer, device_id_type=MESH)

    inverse_loads, couple_loads = [], []
    for m in range(walls):
        source = w
        for b in wall_bits:
            if m & b:
                source = flip(source, b)
        there = pl.ds(pl.multiple_of(source * rows, rows), rows)
        here = pl.ds(m * rows, rows)
        inverse_loads.append(pltpu.make_async_copy(
            inverse.at[:, :, there], inverse_v.at[:, :, here], load_sem.at[1 + m]
        ))
        for at, matrix in enumerate((up, down)):
            couple_loads.append(pltpu.make_async_copy(
                matrix.at[:, :, there], couple_v.at[at, :, :, here],
                load_sem.at[1 + walls * (1 + at) + m],
            ))
    for copy in inverse_loads + couple_loads:
        copy.start()

    def hop(g, c, m, bit):
        return pltpu.make_async_remote_copy(
            src_ref=pieces.at[g, c, m], dst_ref=pieces.at[g, c, m + bit],
            send_sem=send_sem.at[g, c, m + bit], recv_sem=recv_sem.at[g, c, m + bit],
            device_id={"wall": flip(w, bit)}, device_id_type=MESH,
        )

    def arrival(g, c, m):
        low = m & -m
        return hop(g, c, m - low, low)

    def send_own(g, c):
        for bit in reversed(wall_bits):
            hop(g, c, 0, bit).start()

    relayed = sorted(range(2, walls, 2), key=lambda m: -(m & -m))
    spans = {
        "near": [(0, min(2, walls))],
        "mid": [(m, m + 1) for m in range(2, walls, 2)],
        "far": [(m, m + 1) for m in range(3, walls, 2)],
    }

    def collect(part, g, c):
        if part == "near":
            if walls > 1:
                arrival(g, c, 1).wait_recv()
        elif part == "mid":
            for m in relayed:
                arrival(g, c, m).wait_recv()
                for bit in reversed(wall_bits):
                    if bit < (m & -m):
                        hop(g, c, m, bit).start()
        else:
            for m in range(3, walls, 2):
                arrival(g, c, m).wait_recv()

    def times(matrix, g, c, low, high):
        piece = pieces[g, c, low:high].reshape((high - low) * rows, width)
        return jnp.dot(
            matrix[:, low * rows : high * rows], piece, preferred_element_type=jnp.float32
        )

    def halo(s, side, c):
        return pltpu.make_async_remote_copy(
            src_ref=halo_out.at[s, side, c], dst_ref=halo_in.at[s, side, c],
            send_sem=halo_send.at[s, side, c], recv_sem=halo_recv.at[s, side, c],
            device_id={"harm": prev if side == 0 else following}, device_id_type=MESH,
        )

    def start(c):
        tile = None
        for h in range(count):
            turn = (h - c) % count * lanes
            source = sketch_v[h].astype(jnp.float32)
            source = source if turn == 0 else pltpu.roll(source, turn, 1)
            tile = source if tile is None else jnp.where(lane < h * lanes, tile, source)
        pieces[0, c, 0] = tile.astype(jnp.bfloat16)
        send_own(0, c)

    def couple(part, s, c):
        g = 2 * s + 1
        collect(part, g, c)
        if part == "near":
            inner = pieces[0, c, 0].astype(jnp.float32)
        else:
            inner = local[c]
        shifts = [(strip[j] + 1) * lanes for j in range(BAND)]
        for side in (1, 0):
            outer = jnp.zeros((rows, width), jnp.float32) if part == "near" else away[side, c]
            for j in range(BAND):
                if side == 1:
                    turn, stays = lax.rem(shifts[j], width), lane >= shifts[j]
                else:
                    turn, stays = width - shifts[j], lane < width - shifts[j]
                for low, high in spans[part]:
                    product = times(couple_v.at[1 - side, j], g, c, low, high)
                    product = pltpu.roll(product, turn, 1)
                    inner = inner - jnp.where(stays, product, 0.0)
                    outer = outer + jnp.where(stays, 0.0, product)
            if part == "far":
                halo_out[s, side, c] = outer.astype(jnp.bfloat16)
                halo(s, side, c).start()
            else:
                away[side, c] = outer
        local[c] = inner

    def correct(s, c):
        rhs = local[c]
        for side in (1, 0):
            halo(s, side, c).wait_recv()
            rhs = rhs - halo_in[s, side, c].astype(jnp.float32)
        pieces[2 * s + 2, c, 0] = rhs.astype(jnp.bfloat16)
        send_own(2 * s + 2, c)

    def solve(part, s, c):
        g = 2 * s + 2
        collect(part, g, c)
        total = None
        for low, high in spans[part]:
            result = None
            for h in range(count):
                product = times(inverse_v.at[h], g, c, low, high)
                result = product if result is None else jnp.where(lane < h * lanes, result, product)
            total = result if total is None else total + result
        if part != "near":
            total = solved[c] + total
        if part == "far":
            @pl.when(s < SWEEPS - 1)
            def _():
                pieces[g + 1, c, 0] = total.astype(jnp.bfloat16)
                send_own(g + 1, c)
        solved[c] = total

    def take(steps, s):
        for name, c, lag in steps:
            kind, _, part = name.partition(" ")
            if kind == "couple":
                couple(part, s, c)
            elif kind == "correct":
                correct(s, c)
            else:
                solve(part, s - lag, c)

    pl.semaphore_wait(barrier, len(greet))
    own_copy.wait()
    for c in range(count):
        start(c)
    strip_copy.wait()
    for copy in inverse_loads:
        copy.wait()
    steps = steps_of(count)
    solves = [step for step in steps if step[0].startswith("solve")]
    take([step for step in solves if step[2] == 0], -1)
    for copy in couple_loads:
        copy.wait()
    pl.loop(0, SWEEPS)(lambda s: take(steps, s))
    take([step for step in solves if step[2] == 1], SWEEPS)

    out_copies = [
        pltpu.make_async_copy(sampled_v.at[h], sampled.at[h], load_sem.at[2 + 3 * walls + h])
        for h in range(count)
    ]
    total = jnp.zeros((width, width), jnp.float32)
    for h in range(count):
        tile = None
        for c in range(count):
            turn = (c - h) % count * lanes
            source = solved[c] if turn == 0 else pltpu.roll(solved[c], turn, 1)
            tile = source if tile is None else jnp.where(lane < c * lanes, tile, source)
        sampled_v[h] = tile
        out_copies[h].start()
        total = total + lax.dot_general(
            tile, tile, (((0,), (0,)), ((), ())),
            precision=lax.Precision.HIGHEST, preferred_element_type=jnp.float32,
        )

    part = width // 2
    mine, theirs = (w % 2) * part, (1 - w % 2) * part

    def swap(stage, source, target, peer):
        copy = pltpu.make_async_remote_copy(
            src_ref=source, dst_ref=target, send_sem=gram_send.at[stage],
            recv_sem=gram_recv.at[stage], device_id=peer, device_id_type=MESH,
        )
        copy.start()
        return copy

    whole[...] = total
    swap(
        0, whole.at[pl.ds(pl.multiple_of(theirs, part), part)], gram_in.at[0], {"wall": flip(w, 1)}
    ).wait()
    half = whole[pl.ds(pl.multiple_of(mine, part), part), :] + gram_in[0]
    stage = 1
    for axis, peer in butterfly:
        gram_out[stage] = half
        swap(stage, gram_out.at[stage], gram_in.at[stage], {axis: peer}).wait()
        half = half + gram_in[stage]
        stage += 1
    me = z % near
    gathered[me] = half
    copies = [
        swap(stage + d - 1, gathered.at[me], gathered.at[me], {"harm": z - me + (me + d) % near})
        for d in range(1, near)
    ]
    for copy in copies:
        copy.wait()
    half = gathered[0]
    for d in range(1, near):
        half = half + gathered[d]
    stage += near - 1
    half = half / (harms * walls * count * rows)
    place = pl.ds(pl.multiple_of(mine, part), part)
    summed[place, :] = half
    swap(stage, summed.at[place], summed.at[place], {"wall": flip(w, 1)}).wait()
    gram[...] = summed[...]

    for copy in out_copies:
        copy.wait()

    @pl.loop(0, 2 * SWEEPS + 1)
    def _(g):
        for c in range(count):
            for m in range(1, walls):
                arrival(g, c, m).wait_send()

    @pl.loop(0, SWEEPS)
    def _(s):
        for c in range(count):
            for side in range(2):
                halo(s, side, c).wait_send()


def factor_kernel(sampled, gram, basis, triangle, sampled_v, basis_v, work, inverse_lower, sems):
    count, rows, width = sampled_v.shape
    panel, block = 32, 16
    loads = [
        pltpu.make_async_copy(sampled.at[h], sampled_v.at[h], sems.at[0, h]) for h in range(count)
    ]
    stores = [pltpu.make_async_copy(basis_v.at[h], basis.at[h], sems.at[1, h]) for h in range(count)]
    for copy in loads:
        copy.start()
    row_at = lax.broadcasted_iota(jnp.int32, (width, width), 0)
    col_at = lax.broadcasted_iota(jnp.int32, (width, width), 1)
    at = lax.broadcasted_iota(jnp.int32, (panel, width), 0)
    work[...] = gram[...]
    inverse_lower[...] = jnp.where(row_at == col_at, 1.0, 0.0)

    def spread(value, i):
        return jnp.broadcast_to(value[i : i + 1, :], (panel, width))

    for low in range(0, width, panel):
        a = work[low : low + panel, :]
        x = inverse_lower[low : low + panel, :]
        pivots = jnp.ones((panel, width), jnp.float32)
        for first in range(0, panel, block):
            columns = {
                i: jnp.broadcast_to(a[:, low + i : low + i + 1], (panel, width))
                for i in range(first, first + block)
            }
            for i in range(first, first + block):
                pivot = spread(columns[i], i)
                pivots = jnp.where(at == i, pivot, pivots)
                factor = jnp.where(at > i, columns[i] * (1.0 / pivot), 0.0)
                for m in range(i + 1, first + block):
                    columns[m] = columns[m] - factor * spread(columns[m], i)
                a = a - factor * spread(a, i)
                x = x - factor * spread(x, i)
        unit = lax.rsqrt(pivots)
        a, x = a * unit, x * unit
        work[low : low + panel, :] = a
        inverse_lower[low : low + panel, :] = x
        if low + panel < width:
            change = lax.dot_general(
                a, jnp.concatenate([a, x], axis=1), (((0,), (0,)), ((), ())),
                precision=lax.Precision.HIGHEST, preferred_element_type=jnp.float32,
            )
            below = low + panel
            work[below:, :] = work[below:, :] - change[below:, :width]
            inverse_lower[below:, :] = inverse_lower[below:, :] - change[below:, width:]

    for h in range(count):
        loads[h].wait()
        basis_v[h] = lax.dot_general(
            sampled_v[h], inverse_lower[...], (((1,), (1,)), ((), ())),
            precision=lax.Precision.HIGHEST, preferred_element_type=jnp.float32,
        )
        stores[h].start()
    triangle[...] = jnp.where(row_at <= col_at, work[...], 0.0)
    for copy in stores:
        copy.wait()


def body(walls, harms, sketch, inverse_blocks, couple_up, couple_down, strip_harmonics):
    count, rows, width = sketch.shape
    size = rows * walls
    near = min(4, harms)
    stages = len(bits_of(walls)) + len(bits_of(harms // near)) + near
    gathers = 1 + 2 * SWEEPS
    vmem = pl.BlockSpec(memory_space=pltpu.VMEM)
    anywhere = pl.BlockSpec(memory_space=pl.ANY)
    sampled, gram = pl.pallas_call(
        functools.partial(sweep_kernel, walls, harms),
        out_shape=(
            jax.ShapeDtypeStruct((count, rows, width), jnp.float32),
            jax.ShapeDtypeStruct((width, width), jnp.float32),
        ),
        in_specs=[anywhere] * 5,
        out_specs=(anywhere, vmem),
        scratch_shapes=[
            pltpu.SMEM((BAND,), jnp.int32),
            pltpu.VMEM((count, rows, width), jnp.float32),
            pltpu.VMEM((count, rows, width), jnp.bfloat16),
            pltpu.VMEM((gathers, count, walls, rows, width), jnp.bfloat16),
            pltpu.VMEM((count, rows, size), jnp.bfloat16),
            pltpu.VMEM((2, BAND, rows, size), jnp.bfloat16),
            pltpu.VMEM((count, rows, width), jnp.float32),
            pltpu.VMEM((count, rows, width), jnp.float32),
            pltpu.VMEM((2, count, rows, width), jnp.float32),
            pltpu.VMEM((SWEEPS, 2, count, rows, width), jnp.bfloat16),
            pltpu.VMEM((SWEEPS, 2, count, rows, width), jnp.bfloat16),
            pltpu.VMEM((width, width), jnp.float32),
            pltpu.VMEM((width, width), jnp.float32),
            pltpu.VMEM((near, width // 2, width), jnp.float32),
            pltpu.VMEM((stages, width // 2, width), jnp.float32),
            pltpu.VMEM((stages, width // 2, width), jnp.float32),
            pltpu.SemaphoreType.DMA((2 + 3 * walls + count,)),
            pltpu.SemaphoreType.DMA((gathers, count, walls)),
            pltpu.SemaphoreType.DMA((gathers, count, walls)),
            pltpu.SemaphoreType.DMA((SWEEPS, 2, count)),
            pltpu.SemaphoreType.DMA((SWEEPS, 2, count)),
            pltpu.SemaphoreType.DMA((stages,)),
            pltpu.SemaphoreType.DMA((stages,)),
        ],
        compiler_params=pltpu.CompilerParams(
            collective_id=0, has_side_effects=True, vmem_limit_bytes=67043328
        ),
        name="sweeps",
    )(strip_harmonics, sketch, inverse_blocks, couple_up, couple_down)
    return pl.pallas_call(
        factor_kernel,
        out_shape=(
            jax.ShapeDtypeStruct((count, rows, width), jnp.float32),
            jax.ShapeDtypeStruct((width, width), jnp.float32),
        ),
        in_specs=[anywhere, vmem],
        out_specs=(anywhere, vmem),
        scratch_shapes=[
            pltpu.VMEM((count, rows, width), jnp.float32),
            pltpu.VMEM((count, rows, width), jnp.float32),
            pltpu.VMEM((width, width), jnp.float32),
            pltpu.VMEM((width, width), jnp.float32),
            pltpu.SemaphoreType.DMA((2, count)),
        ],
        name="factor",
    )(sampled, gram)


def solution(mesh):
    return jax.shard_map(
        functools.partial(body, mesh.shape["wall"], mesh.shape["harm"]),
        mesh=mesh,
        in_specs=(
            P(("freq", "harm"), "wall", None),
            P(("freq", "harm"), "wall", None),
            P("freq", "wall", None),
            P("freq", "wall", None),
            P("freq"),
        ),
        out_specs=(P(("freq", "harm"), "wall", None), P("freq", None)),
        check_vma=False,
    )
```

```python
import functools

import jax
import jax.numpy as jnp
from jax import lax
from jax.experimental import pallas as pl
from jax.experimental.pallas import tpu as pltpu
from jax.sharding import PartitionSpec as P

BAND = 4
SWEEPS = 3
MESH = pl.DeviceIdType.MESH


def flip(index, bit):
    return index + bit - 2 * bit * (lax.div(index, bit) % 2)


def bits_of(count):
    return [1 << b for b in range(count.bit_length() - 1)]


STEPS = (
    ("couple near", 0, 0), ("couple mid", 0, 0), ("solve mid", 2, 1), ("solve near", 3, 1),
    ("couple far", 0, 0), ("solve far", 2, 1), ("couple near", 1, 0), ("couple mid", 1, 0),
    ("solve mid", 3, 1), ("couple far", 1, 0), ("solve far", 3, 1), ("couple near", 2, 0),
    ("couple mid", 2, 0), ("couple near", 3, 0), ("couple far", 2, 0), ("correct", 0, 0),
    ("couple mid", 3, 0), ("couple far", 3, 0), ("correct", 1, 0), ("solve near", 0, 0),
    ("solve mid", 0, 0), ("solve near", 1, 0), ("solve far", 0, 0), ("correct", 2, 0),
    ("solve mid", 1, 0), ("solve near", 2, 0), ("solve far", 1, 0), ("correct", 3, 0),
)


def steps_of(count):
    if count == 4:
        return STEPS
    names = ("couple near", "couple mid", "couple far", "correct", "solve near", "solve mid", "solve far")
    return tuple((name, c, 0) for name in names for c in range(count))


def pack(full, packed):
    width = full.shape[0]
    part, quarter = width // 2, width // 4
    row = lax.broadcasted_iota(jnp.int32, (part, width), 0)
    lane = lax.broadcasted_iota(jnp.int32, (part, width), 1)
    left = lane[:quarter] < part
    top, low = full[:part], pltpu.roll(full[part:], part, 1)
    turned = pltpu.roll(top, part, 1)
    packed[0, :quarter] = jnp.where(left, turned[:quarter], top[quarter:])
    mixed = jnp.where(row <= lane, top, low)
    packed[1, :quarter] = jnp.where(left, mixed[:quarter], pltpu.roll(mixed[quarter:], part, 1))
    diagonal = jnp.sum(jnp.where(row == lane, low, 0.0), axis=0, keepdims=True)
    packed[0, quarter:] = jnp.zeros((8, width), jnp.float32)
    packed[1, quarter:] = jnp.broadcast_to(diagonal, (8, width))


def unpack(packed, width):
    part, quarter = width // 2, width // 4
    row = lax.broadcasted_iota(jnp.int32, (part, width), 0)
    lane = lax.broadcasted_iota(jnp.int32, (part, width), 1)
    cross, mixed = packed[0, :quarter], packed[1, :quarter]
    cross = jnp.concatenate([pltpu.roll(cross, part, 1), cross], axis=0)
    mixed = jnp.concatenate([mixed, pltpu.roll(mixed, part, 1)], axis=0)
    diagonal = jnp.broadcast_to(packed[1, quarter : quarter + 1], (part, width))
    top = jnp.where(lane < part, jnp.where(row <= lane, mixed, 0.0), cross)
    low = jnp.where(row > lane, mixed, jnp.where(row == lane, diagonal, 0.0))
    once = jnp.concatenate([top, pltpu.roll(low, part, 1)], axis=0)
    row = lax.broadcasted_iota(jnp.int32, (width, width), 0)
    lane = lax.broadcasted_iota(jnp.int32, (width, width), 1)
    return jnp.where(row == lane, once, once + once.T)


def sweep_kernel(
    walls, harms, strip_in, sketch, inverse, up, down, sampled, gram,
    strip, sampled_v, sketch_v, pieces, inverse_v, couple_v, solved, local, away, halo_out, halo_in,
    packed, summed, gathered, gram_out, gram_in,
    load_sem, recv_sem, send_sem, halo_send, halo_recv, gram_send, gram_recv,
):
    count, rows, width = sketch.shape
    lanes = width // count
    w = lax.axis_index("wall")
    z = lax.axis_index("harm")
    prev, following = (z + harms - 1) % harms, (z + 1) % harms
    wall_bits, harm_bits = bits_of(walls), bits_of(harms)
    lane = lax.broadcasted_iota(jnp.int32, (rows, width), 1)

    near = min(4, harms)
    butterfly = [("wall", flip(w, b)) for b in wall_bits if b > 2]
    butterfly += [("harm", flip(z, b)) for b in harm_bits if b >= near]
    greet = [{"wall": flip(w, b)} for b in wall_bits]
    greet += [{"harm": flip(z, b)} for b in harm_bits if b >= near]
    greet += [{"harm": prev}, {"harm": following}]
    direct = []
    for across in range(2):
        for d in range(near):
            peer = {"harm": z - z % near + (z % near + d) % near} if d else {}
            peer.update({"wall": flip(w, 2)} if across else {})
            direct += [peer] if peer else []
    barrier = pltpu.get_barrier_semaphore()

    own_copy = pltpu.make_async_copy(sketch, sketch_v, load_sem.at[0])
    own_copy.start()
    strip_copy = pltpu.make_async_copy(strip_in, strip, load_sem.at[1 + 3 * walls])
    strip_copy.start()
    for peer in greet:
        pl.semaphore_signal(barrier, inc=1, device_id=peer, device_id_type=MESH)

    inverse_loads, couple_loads = [], []
    for m in range(walls):
        source = w
        for b in wall_bits:
            if m & b:
                source = flip(source, b)
        there = pl.ds(pl.multiple_of(source * rows, rows), rows)
        here = pl.ds(m * rows, rows)
        inverse_loads.append(pltpu.make_async_copy(
            inverse.at[:, :, there], inverse_v.at[:, :, here], load_sem.at[1 + m]
        ))
        for at, matrix in enumerate((up, down)):
            couple_loads.append(pltpu.make_async_copy(
                matrix.at[:, :, there], couple_v.at[at, :, :, here],
                load_sem.at[1 + walls * (1 + at) + m],
            ))
    for copy in inverse_loads + couple_loads:
        copy.start()

    def hop(g, c, m, bit):
        return pltpu.make_async_remote_copy(
            src_ref=pieces.at[g, c, m], dst_ref=pieces.at[g, c, m + bit],
            send_sem=send_sem.at[g, c, m + bit], recv_sem=recv_sem.at[g, c, m + bit],
            device_id={"wall": flip(w, bit)}, device_id_type=MESH,
        )

    def arrival(g, c, m):
        low = m & -m
        return hop(g, c, m - low, low)

    def send_own(g, c):
        for bit in reversed(wall_bits):
            hop(g, c, 0, bit).start()

    relayed = sorted(range(2, walls, 2), key=lambda m: -(m & -m))
    spans = {
        "near": [(0, min(2, walls))],
        "mid": [(m, m + 1) for m in range(2, walls, 2)],
        "far": [(m, m + 1) for m in range(3, walls, 2)],
    }

    def collect(part, g, c):
        if part == "near":
            if walls > 1:
                arrival(g, c, 1).wait_recv()
        elif part == "mid":
            for m in relayed:
                arrival(g, c, m).wait_recv()
                for bit in reversed(wall_bits):
                    if bit < (m & -m):
                        hop(g, c, m, bit).start()
        else:
            for m in range(3, walls, 2):
                arrival(g, c, m).wait_recv()

    def times(matrix, g, c, low, high):
        piece = pieces[g, c, low:high].reshape((high - low) * rows, width)
        return jnp.dot(
            matrix[:, low * rows : high * rows], piece, preferred_element_type=jnp.float32
        )

    def halo(s, side, c):
        return pltpu.make_async_remote_copy(
            src_ref=halo_out.at[s, side, c], dst_ref=halo_in.at[s, side, c],
            send_sem=halo_send.at[s, side, c], recv_sem=halo_recv.at[s, side, c],
            device_id={"harm": prev if side == 0 else following}, device_id_type=MESH,
        )

    def start(c):
        tile = None
        for h in range(count):
            turn = (h - c) % count * lanes
            source = sketch_v[h].astype(jnp.float32)
            source = source if turn == 0 else pltpu.roll(source, turn, 1)
            tile = source if tile is None else jnp.where(lane < h * lanes, tile, source)
        pieces[0, c, 0] = tile.astype(jnp.bfloat16)

    def couple(part, s, c):
        g = 2 * s + 1
        collect(part, g, c)
        if part == "near":
            inner = pieces[0, c, 0].astype(jnp.float32)
        else:
            inner = local[c]
        shifts = [(strip[j] + 1) * lanes for j in range(BAND)]
        for side in (1, 0):
            outer = jnp.zeros((rows, width), jnp.float32) if part == "near" else away[side, c]
            for j in range(BAND):
                if side == 1:
                    turn, stays = lax.rem(shifts[j], width), lane >= shifts[j]
                else:
                    turn, stays = width - shifts[j], lane < width - shifts[j]
                for low, high in spans[part]:
                    product = times(couple_v.at[1 - side, j], g, c, low, high)
                    product = pltpu.roll(product, turn, 1)
                    inner = inner - jnp.where(stays, product, 0.0)
                    outer = outer + jnp.where(stays, 0.0, product)
            if part == "far":
                halo_out[s, side, c] = outer.astype(jnp.bfloat16)
                halo(s, side, c).start()
            else:
                away[side, c] = outer
        local[c] = inner

    def correct(s, c):
        rhs = local[c]
        for side in (1, 0):
            halo(s, side, c).wait_recv()
            rhs = rhs - halo_in[s, side, c].astype(jnp.float32)
        pieces[2 * s + 2, c, 0] = rhs.astype(jnp.bfloat16)
        send_own(2 * s + 2, c)

    def solve(part, s, c):
        g = 2 * s + 2
        collect(part, g, c)
        total = None
        for low, high in spans[part]:
            result = None
            for h in range(count):
                product = times(inverse_v.at[h], g, c, low, high)
                result = product if result is None else jnp.where(lane < h * lanes, result, product)
            total = result if total is None else total + result
        if part != "near":
            total = solved[c] + total
        if part == "far":
            @pl.when(s < SWEEPS - 1)
            def _():
                pieces[g + 1, c, 0] = total.astype(jnp.bfloat16)
                send_own(g + 1, c)
        solved[c] = total

    def take(steps, s):
        for name, c, lag in steps:
            kind, _, part = name.partition(" ")
            if kind == "couple":
                couple(part, s, c)
            elif kind == "correct":
                correct(s, c)
            else:
                solve(part, s - lag, c)

    own_copy.wait()
    for c in range(count):
        start(c)
    pl.semaphore_wait(barrier, len(greet))
    for c in range(count):
        send_own(0, c)
    strip_copy.wait()
    for copy in inverse_loads:
        copy.wait()
    steps = steps_of(count)
    solves = [step for step in steps if step[0].startswith("solve")]
    take([step for step in solves if step[2] == 0], -1)
    for copy in couple_loads:
        copy.wait()
    pl.loop(0, SWEEPS)(lambda s: take(steps, s))
    take([step for step in solves if step[2] == 1], SWEEPS)

    out_copies = [
        pltpu.make_async_copy(sampled_v.at[h], sampled.at[h], load_sem.at[2 + 3 * walls + h])
        for h in range(count)
    ]
    total = jnp.zeros((width, width), jnp.float32)
    for h in range(count):
        tile = None
        for c in range(count):
            turn = (c - h) % count * lanes
            source = solved[c] if turn == 0 else pltpu.roll(solved[c], turn, 1)
            tile = source if tile is None else jnp.where(lane < c * lanes, tile, source)
        sampled_v[h] = tile
        out_copies[h].start()
        total = total + lax.dot_general(
            tile, tile, (((0,), (0,)), ((), ())),
            precision=lax.Precision.HIGHEST, preferred_element_type=jnp.float32,
        )

    def swap(stage, source, target, peer):
        copy = pltpu.make_async_remote_copy(
            src_ref=source, dst_ref=target, send_sem=gram_send.at[stage],
            recv_sem=gram_recv.at[stage], device_id=peer, device_id_type=MESH,
        )
        copy.start()
        return copy

    side = w % 2
    pack(total, packed)
    swap(0, packed.at[1 - side], gram_in.at[0], {"wall": flip(w, 1)}).wait()
    half = packed[side] + gram_in[0]
    stage = 1
    for axis, peer in butterfly:
        gram_out[stage] = half
        swap(stage, gram_out.at[stage], gram_in.at[stage], {axis: peer}).wait()
        half = half + gram_in[stage]
        stage += 1
    me = lax.div(w, 2) % 2 * near + z % near
    gathered[me] = half
    copies = [
        swap(stage + at, gathered.at[me], gathered.at[me], peer)
        for at, peer in enumerate(direct)
    ]
    for copy in copies:
        copy.wait()
    half = gathered[0]
    for slot in range(1, len(direct) + 1):
        half = half + gathered[slot]
    stage += len(direct)
    summed[side] = half / (harms * walls * count * rows)
    swap(stage, summed.at[side], summed.at[side], {"wall": flip(w, 1)}).wait()
    gram[...] = unpack(summed, width)

    for copy in out_copies:
        copy.wait()

    @pl.loop(0, 2 * SWEEPS + 1)
    def _(g):
        for c in range(count):
            for m in range(1, walls):
                arrival(g, c, m).wait_send()

    @pl.loop(0, SWEEPS)
    def _(s):
        for c in range(count):
            for side in range(2):
                halo(s, side, c).wait_send()


def factor_kernel(sampled, gram, basis, triangle, sampled_v, basis_v, work, inverse_lower, sems):
    count, rows, width = sampled_v.shape
    panel, block = 32, 16
    loads = [
        pltpu.make_async_copy(sampled.at[h], sampled_v.at[h], sems.at[0, h]) for h in range(count)
    ]
    stores = [pltpu.make_async_copy(basis_v.at[h], basis.at[h], sems.at[1, h]) for h in range(count)]
    for copy in loads:
        copy.start()
    row_at = lax.broadcasted_iota(jnp.int32, (width, width), 0)
    col_at = lax.broadcasted_iota(jnp.int32, (width, width), 1)
    at = lax.broadcasted_iota(jnp.int32, (panel, width), 0)
    work[...] = gram[...]
    inverse_lower[...] = jnp.where(row_at == col_at, 1.0, 0.0)

    def spread(value, i):
        return jnp.broadcast_to(value[i : i + 1, :], (panel, width))

    for low in range(0, width, panel):
        a = work[low : low + panel, :]
        x = inverse_lower[low : low + panel, :]
        pivots = jnp.ones((panel, width), jnp.float32)
        for first in range(0, panel, block):
            columns = {
                i: jnp.broadcast_to(a[:, low + i : low + i + 1], (panel, width))
                for i in range(first, first + block)
            }
            for i in range(first, first + block):
                pivot = spread(columns[i], i)
                pivots = jnp.where(at == i, pivot, pivots)
                factor = jnp.where(at > i, columns[i] * (1.0 / pivot), 0.0)
                for m in range(i + 1, first + block):
                    columns[m] = columns[m] - factor * spread(columns[m], i)
                a = a - factor * spread(a, i)
                x = x - factor * spread(x, i)
        unit = lax.rsqrt(pivots)
        a, x = a * unit, x * unit
        work[low : low + panel, :] = a
        inverse_lower[low : low + panel, :] = x
        if low + panel < width:
            change = lax.dot_general(
                a, jnp.concatenate([a, x], axis=1), (((0,), (0,)), ((), ())),
                precision=lax.Precision.HIGHEST, preferred_element_type=jnp.float32,
            )
            below = low + panel
            work[below:, :] = work[below:, :] - change[below:, :width]
            inverse_lower[below:, :] = inverse_lower[below:, :] - change[below:, width:]

    for h in range(count):
        loads[h].wait()
        basis_v[h] = lax.dot_general(
            sampled_v[h], inverse_lower[...], (((1,), (1,)), ((), ())),
            precision=lax.Precision.HIGHEST, preferred_element_type=jnp.float32,
        )
        stores[h].start()
    triangle[...] = jnp.where(row_at <= col_at, work[...], 0.0)
    for copy in stores:
        copy.wait()


def body(walls, harms, sketch, inverse_blocks, couple_up, couple_down, strip_harmonics):
    count, rows, width = sketch.shape
    size = rows * walls
    near = min(4, harms)
    stages = len(bits_of(walls)) + len(bits_of(harms // near)) + 2 * near
    short = width // 4 + 8
    gathers = 1 + 2 * SWEEPS
    vmem = pl.BlockSpec(memory_space=pltpu.VMEM)
    anywhere = pl.BlockSpec(memory_space=pl.ANY)
    sampled, gram = pl.pallas_call(
        functools.partial(sweep_kernel, walls, harms),
        out_shape=(
            jax.ShapeDtypeStruct((count, rows, width), jnp.float32),
            jax.ShapeDtypeStruct((width, width), jnp.float32),
        ),
        in_specs=[anywhere] * 5,
        out_specs=(anywhere, vmem),
        scratch_shapes=[
            pltpu.SMEM((BAND,), jnp.int32),
            pltpu.VMEM((count, rows, width), jnp.float32),
            pltpu.VMEM((count, rows, width), jnp.bfloat16),
            pltpu.VMEM((gathers, count, walls, rows, width), jnp.bfloat16),
            pltpu.VMEM((count, rows, size), jnp.bfloat16),
            pltpu.VMEM((2, BAND, rows, size), jnp.bfloat16),
            pltpu.VMEM((count, rows, width), jnp.float32),
            pltpu.VMEM((count, rows, width), jnp.float32),
            pltpu.VMEM((2, count, rows, width), jnp.float32),
            pltpu.VMEM((SWEEPS, 2, count, rows, width), jnp.bfloat16),
            pltpu.VMEM((SWEEPS, 2, count, rows, width), jnp.bfloat16),
            pltpu.VMEM((2, short, width), jnp.float32),
            pltpu.VMEM((2, short, width), jnp.float32),
            pltpu.VMEM((2 * near, short, width), jnp.float32),
            pltpu.VMEM((stages, short, width), jnp.float32),
            pltpu.VMEM((stages, short, width), jnp.float32),
            pltpu.SemaphoreType.DMA((2 + 3 * walls + count,)),
            pltpu.SemaphoreType.DMA((gathers, count, walls)),
            pltpu.SemaphoreType.DMA((gathers, count, walls)),
            pltpu.SemaphoreType.DMA((SWEEPS, 2, count)),
            pltpu.SemaphoreType.DMA((SWEEPS, 2, count)),
            pltpu.SemaphoreType.DMA((stages,)),
            pltpu.SemaphoreType.DMA((stages,)),
        ],
        compiler_params=pltpu.CompilerParams(
            collective_id=0, has_side_effects=True, vmem_limit_bytes=67043328
        ),
        name="sweeps",
    )(strip_harmonics, sketch, inverse_blocks, couple_up, couple_down)
    return pl.pallas_call(
        factor_kernel,
        out_shape=(
            jax.ShapeDtypeStruct((count, rows, width), jnp.float32),
            jax.ShapeDtypeStruct((width, width), jnp.float32),
        ),
        in_specs=[anywhere, vmem],
        out_specs=(anywhere, vmem),
        scratch_shapes=[
            pltpu.VMEM((count, rows, width), jnp.float32),
            pltpu.VMEM((count, rows, width), jnp.float32),
            pltpu.VMEM((width, width), jnp.float32),
            pltpu.VMEM((width, width), jnp.float32),
            pltpu.SemaphoreType.DMA((2, count)),
        ],
        name="factor",
    )(sampled, gram)


def solution(mesh):
    return jax.shard_map(
        functools.partial(body, mesh.shape["wall"], mesh.shape["harm"]),
        mesh=mesh,
        in_specs=(
            P(("freq", "harm"), "wall", None),
            P(("freq", "harm"), "wall", None),
            P("freq", "wall", None),
            P("freq", "wall", None),
            P("freq"),
        ),
        out_specs=(P(("freq", "harm"), "wall", None), P("freq", None)),
        check_vma=False,
    )
```

```python
import functools

import jax
import jax.numpy as jnp
from jax import lax
from jax.experimental import pallas as pl
from jax.experimental.pallas import tpu as pltpu
from jax.sharding import PartitionSpec as P

BAND = 4
SWEEPS = 3
MESH = pl.DeviceIdType.MESH


def flip(index, bit):
    return index + bit - 2 * bit * (lax.div(index, bit) % 2)


def bits_of(count):
    return [1 << b for b in range(count.bit_length() - 1)]


STEPS = (
    ("couple near", 0, 0), ("couple mid", 0, 0), ("solve mid", 2, 1), ("solve near", 3, 1),
    ("couple far", 0, 0), ("solve far", 2, 1), ("couple near", 1, 0), ("couple mid", 1, 0),
    ("solve mid", 3, 1), ("couple far", 1, 0), ("solve far", 3, 1), ("couple near", 2, 0),
    ("couple mid", 2, 0), ("couple near", 3, 0), ("couple far", 2, 0), ("correct", 0, 0),
    ("couple mid", 3, 0), ("couple far", 3, 0), ("correct", 1, 0), ("solve near", 0, 0),
    ("solve mid", 0, 0), ("solve near", 1, 0), ("solve far", 0, 0), ("correct", 2, 0),
    ("solve mid", 1, 0), ("solve near", 2, 0), ("solve far", 1, 0), ("correct", 3, 0),
)


def steps_of(count):
    if count == 4:
        return STEPS
    names = ("couple near", "couple mid", "couple far", "correct", "solve near", "solve mid", "solve far")
    return tuple((name, c, 0) for name in names for c in range(count))


def pack(full, packed):
    width = full.shape[0]
    part, quarter = width // 2, width // 4
    row = lax.broadcasted_iota(jnp.int32, (part, width), 0)
    lane = lax.broadcasted_iota(jnp.int32, (part, width), 1)
    left = lane[:quarter] < part
    top, low = full[:part], pltpu.roll(full[part:], part, 1)
    turned = pltpu.roll(top, part, 1)
    packed[0, :quarter] = jnp.where(left, turned[:quarter], top[quarter:])
    mixed = jnp.where(row <= lane, top, low)
    packed[1, :quarter] = jnp.where(left, mixed[:quarter], pltpu.roll(mixed[quarter:], part, 1))
    diagonal = jnp.sum(jnp.where(row == lane, low, 0.0), axis=0, keepdims=True)
    packed[0, quarter:] = jnp.zeros((8, width), jnp.float32)
    packed[1, quarter:] = jnp.broadcast_to(diagonal, (8, width))


def unpack(packed, width):
    part, quarter = width // 2, width // 4
    row = lax.broadcasted_iota(jnp.int32, (part, width), 0)
    lane = lax.broadcasted_iota(jnp.int32, (part, width), 1)
    cross, mixed = packed[0, :quarter], packed[1, :quarter]
    cross = jnp.concatenate([pltpu.roll(cross, part, 1), cross], axis=0)
    mixed = jnp.concatenate([mixed, pltpu.roll(mixed, part, 1)], axis=0)
    diagonal = jnp.broadcast_to(packed[1, quarter : quarter + 1], (part, width))
    top = jnp.where(lane < part, jnp.where(row <= lane, mixed, 0.0), cross)
    low = jnp.where(row > lane, mixed, jnp.where(row == lane, diagonal, 0.0))
    once = jnp.concatenate([top, pltpu.roll(low, part, 1)], axis=0)
    row = lax.broadcasted_iota(jnp.int32, (width, width), 0)
    lane = lax.broadcasted_iota(jnp.int32, (width, width), 1)
    return jnp.where(row == lane, once, once + once.T)


def sweep_kernel(
    walls, harms, strip_in, sketch, inverse, up, down, sampled, gram,
    strip, sampled_v, sketch_v, pieces, inverse_v, couple_v, solved, local, away, halo_out, halo_in,
    packed, summed, gathered, gram_out, gram_in,
    load_sem, recv_sem, send_sem, halo_send, halo_recv, gram_send, gram_recv, word,
):
    count, rows, width = sketch.shape
    lanes = width // count
    w = lax.axis_index("wall")
    z = lax.axis_index("harm")
    prev, following = (z + harms - 1) % harms, (z + 1) % harms
    wall_bits, harm_bits = bits_of(walls), bits_of(harms)
    lane = lax.broadcasted_iota(jnp.int32, (rows, width), 1)

    near = min(4, harms)
    butterfly = [("wall", flip(w, b)) for b in wall_bits if b > 2]
    butterfly += [("harm", flip(z, b)) for b in harm_bits if b >= near]
    greet = [{"wall": flip(w, b)} for b in wall_bits]
    greet += [{"harm": flip(z, b)} for b in harm_bits if b >= near]
    if harms < 3:
        greet += [{"harm": prev}, {"harm": following}]
    direct = []
    for across in range(2):
        for d in range(near):
            peer = {"harm": z - z % near + (z % near + d) % near} if d else {}
            peer.update({"wall": flip(w, 2)} if across else {})
            direct += [peer] if peer else []
    barrier = pltpu.get_barrier_semaphore()

    own_copy = pltpu.make_async_copy(sketch, sketch_v, load_sem.at[0])
    own_copy.start()
    strip_copy = pltpu.make_async_copy(strip_in, strip, load_sem.at[1 + 3 * walls])
    strip_copy.start()
    for peer in greet:
        pl.semaphore_signal(barrier, inc=1, device_id=peer, device_id_type=MESH)

    def tell(semaphore, peer):
        pl.semaphore_signal(semaphore, inc=1, device_id={"harm": peer}, device_id_type=MESH)

    heard = len(greet)
    if harms > 2:
        pl.when(z > 0)(lambda: tell(barrier, prev))
        pl.when(z < harms - 1)(lambda: tell(barrier, following))
        heard = heard + (z > 0).astype(jnp.int32) + (z < harms - 1).astype(jnp.int32)

    def first_word():
        pl.when(z == 1)(lambda: tell(word.at[0], following))
        pl.when(z == harms - 2)(lambda: tell(word.at[1], prev))

    def pass_on():
        @pl.when((z > 1) & (z < harms - 1))
        def _():
            pl.semaphore_wait(word.at[0], 1)
            tell(word.at[0], following)

        @pl.when((z > 0) & (z < harms - 2))
        def _():
            pl.semaphore_wait(word.at[1], 1)
            tell(word.at[1], prev)

    def last_word():
        pl.when(z == harms - 1)(lambda: pl.semaphore_wait(word.at[0], 1))
        pl.when(z == 0)(lambda: pl.semaphore_wait(word.at[1], 1))


    inverse_loads, couple_loads = [], []
    for m in range(walls):
        source = w
        for b in wall_bits:
            if m & b:
                source = flip(source, b)
        there = pl.ds(pl.multiple_of(source * rows, rows), rows)
        here = pl.ds(m * rows, rows)
        inverse_loads.append(pltpu.make_async_copy(
            inverse.at[:, :, there], inverse_v.at[:, :, here], load_sem.at[1 + m]
        ))
        for at, matrix in enumerate((up, down)):
            couple_loads.append(pltpu.make_async_copy(
                matrix.at[:, :, there], couple_v.at[at, :, :, here],
                load_sem.at[1 + walls * (1 + at) + m],
            ))
    for copy in inverse_loads + couple_loads:
        copy.start()

    def hop(g, c, m, bit):
        return pltpu.make_async_remote_copy(
            src_ref=pieces.at[g, c, m], dst_ref=pieces.at[g, c, m + bit],
            send_sem=send_sem.at[g, c, m + bit], recv_sem=recv_sem.at[g, c, m + bit],
            device_id={"wall": flip(w, bit)}, device_id_type=MESH,
        )

    def arrival(g, c, m):
        low = m & -m
        return hop(g, c, m - low, low)

    def send_own(g, c):
        for bit in reversed(wall_bits):
            hop(g, c, 0, bit).start()

    relayed = sorted(range(2, walls, 2), key=lambda m: -(m & -m))
    spans = {
        "near": [(0, min(2, walls))],
        "mid": [(m, m + 1) for m in range(2, walls, 2)],
        "far": [(m, m + 1) for m in range(3, walls, 2)],
    }

    def collect(part, g, c):
        if part == "near":
            if walls > 1:
                arrival(g, c, 1).wait_recv()
        elif part == "mid":
            for m in relayed:
                arrival(g, c, m).wait_recv()
                for bit in reversed(wall_bits):
                    if bit < (m & -m):
                        hop(g, c, m, bit).start()
        else:
            for m in range(3, walls, 2):
                arrival(g, c, m).wait_recv()

    def times(matrix, g, c, low, high):
        piece = pieces[g, c, low:high].reshape((high - low) * rows, width)
        return jnp.dot(
            matrix[:, low * rows : high * rows], piece, preferred_element_type=jnp.float32
        )

    def halo(s, side, c):
        return pltpu.make_async_remote_copy(
            src_ref=halo_out.at[s, side, c], dst_ref=halo_in.at[s, side, c],
            send_sem=halo_send.at[s, side, c], recv_sem=halo_recv.at[s, side, c],
            device_id={"harm": prev if side == 0 else following}, device_id_type=MESH,
        )

    def start(c):
        tile = None
        for h in range(count):
            turn = (h - c) % count * lanes
            source = sketch_v[h].astype(jnp.float32)
            source = source if turn == 0 else pltpu.roll(source, turn, 1)
            tile = source if tile is None else jnp.where(lane < h * lanes, tile, source)
        pieces[0, c, 0] = tile.astype(jnp.bfloat16)

    def couple(part, s, c):
        g = 2 * s + 1
        collect(part, g, c)
        if part == "near":
            inner = pieces[0, c, 0].astype(jnp.float32)
        else:
            inner = local[c]
        shifts = [(strip[j] + 1) * lanes for j in range(BAND)]
        for side in (1, 0):
            outer = jnp.zeros((rows, width), jnp.float32) if part == "near" else away[side, c]
            for j in range(BAND):
                if side == 1:
                    turn, stays = lax.rem(shifts[j], width), lane >= shifts[j]
                else:
                    turn, stays = width - shifts[j], lane < width - shifts[j]
                for low, high in spans[part]:
                    product = times(couple_v.at[1 - side, j], g, c, low, high)
                    product = pltpu.roll(product, turn, 1)
                    inner = inner - jnp.where(stays, product, 0.0)
                    outer = outer + jnp.where(stays, 0.0, product)
            if part == "far":
                halo_out[s, side, c] = outer.astype(jnp.bfloat16)
                halo(s, side, c).start()
            else:
                away[side, c] = outer
        local[c] = inner

    def correct(s, c):
        rhs = local[c]
        for side in (1, 0):
            halo(s, side, c).wait_recv()
            rhs = rhs - halo_in[s, side, c].astype(jnp.float32)
        pieces[2 * s + 2, c, 0] = rhs.astype(jnp.bfloat16)
        send_own(2 * s + 2, c)

    def solve(part, s, c):
        g = 2 * s + 2
        collect(part, g, c)
        total = None
        for low, high in spans[part]:
            result = None
            for h in range(count):
                product = times(inverse_v.at[h], g, c, low, high)
                result = product if result is None else jnp.where(lane < h * lanes, result, product)
            total = result if total is None else total + result
        if part != "near":
            total = solved[c] + total
        if part == "far":
            @pl.when(s < SWEEPS - 1)
            def _():
                pieces[g + 1, c, 0] = total.astype(jnp.bfloat16)
                send_own(g + 1, c)
        solved[c] = total

    def take(steps, s):
        for name, c, lag in steps:
            kind, _, part = name.partition(" ")
            if kind == "couple":
                couple(part, s, c)
            elif kind == "correct":
                correct(s, c)
            else:
                solve(part, s - lag, c)

    own_copy.wait()
    for c in range(count):
        start(c)
    pl.semaphore_wait(barrier, heard)
    for c in range(count):
        send_own(0, c)
    if harms > 2:
        first_word()
    strip_copy.wait()
    for copy in inverse_loads:
        copy.wait()
    if harms > 2:
        pass_on()
    steps = steps_of(count)
    solves = [step for step in steps if step[0].startswith("solve")]
    take([step for step in solves if step[2] == 0], -1)
    for copy in couple_loads:
        copy.wait()
    if harms > 2:
        last_word()
    pl.loop(0, SWEEPS)(lambda s: take(steps, s))
    take([step for step in solves if step[2] == 1], SWEEPS)

    out_copies = [
        pltpu.make_async_copy(sampled_v.at[h], sampled.at[h], load_sem.at[2 + 3 * walls + h])
        for h in range(count)
    ]
    total = jnp.zeros((width, width), jnp.float32)
    for h in range(count):
        tile = None
        for c in range(count):
            turn = (c - h) % count * lanes
            source = solved[c] if turn == 0 else pltpu.roll(solved[c], turn, 1)
            tile = source if tile is None else jnp.where(lane < c * lanes, tile, source)
        sampled_v[h] = tile
        out_copies[h].start()
        total = total + lax.dot_general(
            tile, tile, (((0,), (0,)), ((), ())),
            precision=lax.Precision.HIGHEST, preferred_element_type=jnp.float32,
        )

    def swap(stage, source, target, peer):
        copy = pltpu.make_async_remote_copy(
            src_ref=source, dst_ref=target, send_sem=gram_send.at[stage],
            recv_sem=gram_recv.at[stage], device_id=peer, device_id_type=MESH,
        )
        copy.start()
        return copy

    side = w % 2
    pack(total, packed)
    swap(0, packed.at[1 - side], gram_in.at[0], {"wall": flip(w, 1)}).wait()
    half = packed[side] + gram_in[0]
    stage = 1
    for axis, peer in butterfly:
        gram_out[stage] = half
        swap(stage, gram_out.at[stage], gram_in.at[stage], {axis: peer}).wait()
        half = half + gram_in[stage]
        stage += 1
    me = lax.div(w, 2) % 2 * near + z % near
    gathered[me] = half
    copies = [
        swap(stage + at, gathered.at[me], gathered.at[me], peer)
        for at, peer in enumerate(direct)
    ]
    for copy in copies:
        copy.wait()
    half = gathered[0]
    for slot in range(1, len(direct) + 1):
        half = half + gathered[slot]
    stage += len(direct)
    summed[side] = half / (harms * walls * count * rows)
    swap(stage, summed.at[side], summed.at[side], {"wall": flip(w, 1)}).wait()
    gram[...] = unpack(summed, width)

    for copy in out_copies:
        copy.wait()

    @pl.loop(0, 2 * SWEEPS + 1)
    def _(g):
        for c in range(count):
            for m in range(1, walls):
                arrival(g, c, m).wait_send()

    @pl.loop(0, SWEEPS)
    def _(s):
        for c in range(count):
            for side in range(2):
                halo(s, side, c).wait_send()


def factor_kernel(sampled, gram, basis, triangle, sampled_v, basis_v, work, inverse_lower, sems):
    count, rows, width = sampled_v.shape
    panel, block = 32, 16
    loads = [
        pltpu.make_async_copy(sampled.at[h], sampled_v.at[h], sems.at[0, h]) for h in range(count)
    ]
    stores = [pltpu.make_async_copy(basis_v.at[h], basis.at[h], sems.at[1, h]) for h in range(count)]
    for copy in loads:
        copy.start()
    row_at = lax.broadcasted_iota(jnp.int32, (width, width), 0)
    col_at = lax.broadcasted_iota(jnp.int32, (width, width), 1)
    at = lax.broadcasted_iota(jnp.int32, (panel, width), 0)
    work[...] = gram[...]
    inverse_lower[...] = jnp.where(row_at == col_at, 1.0, 0.0)

    def spread(value, i):
        return jnp.broadcast_to(value[i : i + 1, :], (panel, width))

    for low in range(0, width, panel):
        a = work[low : low + panel, :]
        x = inverse_lower[low : low + panel, :]
        pivots = jnp.ones((panel, width), jnp.float32)
        for first in range(0, panel, block):
            columns = {
                i: jnp.broadcast_to(a[:, low + i : low + i + 1], (panel, width))
                for i in range(first, first + block)
            }
            for i in range(first, first + block):
                pivot = spread(columns[i], i)
                pivots = jnp.where(at == i, pivot, pivots)
                factor = jnp.where(at > i, columns[i] * (1.0 / pivot), 0.0)
                for m in range(i + 1, first + block):
                    columns[m] = columns[m] - factor * spread(columns[m], i)
                a = a - factor * spread(a, i)
                x = x - factor * spread(x, i)
        unit = lax.rsqrt(pivots)
        a, x = a * unit, x * unit
        work[low : low + panel, :] = a
        inverse_lower[low : low + panel, :] = x
        if low + panel < width:
            change = lax.dot_general(
                a, jnp.concatenate([a, x], axis=1), (((0,), (0,)), ((), ())),
                precision=lax.Precision.HIGHEST, preferred_element_type=jnp.float32,
            )
            below = low + panel
            work[below:, :] = work[below:, :] - change[below:, :width]
            inverse_lower[below:, :] = inverse_lower[below:, :] - change[below:, width:]

    for h in range(count):
        loads[h].wait()
        basis_v[h] = lax.dot_general(
            sampled_v[h], inverse_lower[...], (((1,), (1,)), ((), ())),
            precision=lax.Precision.HIGHEST, preferred_element_type=jnp.float32,
        )
        stores[h].start()
    triangle[...] = jnp.where(row_at <= col_at, work[...], 0.0)
    for copy in stores:
        copy.wait()


def body(walls, harms, sketch, inverse_blocks, couple_up, couple_down, strip_harmonics):
    count, rows, width = sketch.shape
    size = rows * walls
    near = min(4, harms)
    stages = len(bits_of(walls)) + len(bits_of(harms // near)) + 2 * near
    short = width // 4 + 8
    gathers = 1 + 2 * SWEEPS
    vmem = pl.BlockSpec(memory_space=pltpu.VMEM)
    anywhere = pl.BlockSpec(memory_space=pl.ANY)
    sampled, gram = pl.pallas_call(
        functools.partial(sweep_kernel, walls, harms),
        out_shape=(
            jax.ShapeDtypeStruct((count, rows, width), jnp.float32),
            jax.ShapeDtypeStruct((width, width), jnp.float32),
        ),
        in_specs=[anywhere] * 5,
        out_specs=(anywhere, vmem),
        scratch_shapes=[
            pltpu.SMEM((BAND,), jnp.int32),
            pltpu.VMEM((count, rows, width), jnp.float32),
            pltpu.VMEM((count, rows, width), jnp.bfloat16),
            pltpu.VMEM((gathers, count, walls, rows, width), jnp.bfloat16),
            pltpu.VMEM((count, rows, size), jnp.bfloat16),
            pltpu.VMEM((2, BAND, rows, size), jnp.bfloat16),
            pltpu.VMEM((count, rows, width), jnp.float32),
            pltpu.VMEM((count, rows, width), jnp.float32),
            pltpu.VMEM((2, count, rows, width), jnp.float32),
            pltpu.VMEM((SWEEPS, 2, count, rows, width), jnp.bfloat16),
            pltpu.VMEM((SWEEPS, 2, count, rows, width), jnp.bfloat16),
            pltpu.VMEM((2, short, width), jnp.float32),
            pltpu.VMEM((2, short, width), jnp.float32),
            pltpu.VMEM((2 * near, short, width), jnp.float32),
            pltpu.VMEM((stages, short, width), jnp.float32),
            pltpu.VMEM((stages, short, width), jnp.float32),
            pltpu.SemaphoreType.DMA((2 + 3 * walls + count,)),
            pltpu.SemaphoreType.DMA((gathers, count, walls)),
            pltpu.SemaphoreType.DMA((gathers, count, walls)),
            pltpu.SemaphoreType.DMA((SWEEPS, 2, count)),
            pltpu.SemaphoreType.DMA((SWEEPS, 2, count)),
            pltpu.SemaphoreType.DMA((stages,)),
            pltpu.SemaphoreType.DMA((stages,)),
            pltpu.SemaphoreType.REGULAR((2,)),
        ],
        compiler_params=pltpu.CompilerParams(
            collective_id=0, has_side_effects=True, vmem_limit_bytes=67043328
        ),
        name="sweeps",
    )(strip_harmonics, sketch, inverse_blocks, couple_up, couple_down)
    return pl.pallas_call(
        factor_kernel,
        out_shape=(
            jax.ShapeDtypeStruct((count, rows, width), jnp.float32),
            jax.ShapeDtypeStruct((width, width), jnp.float32),
        ),
        in_specs=[anywhere, vmem],
        out_specs=(anywhere, vmem),
        scratch_shapes=[
            pltpu.VMEM((count, rows, width), jnp.float32),
            pltpu.VMEM((count, rows, width), jnp.float32),
            pltpu.VMEM((width, width), jnp.float32),
            pltpu.VMEM((width, width), jnp.float32),
            pltpu.SemaphoreType.DMA((2, count)),
        ],
        name="factor",
    )(sampled, gram)


def solution(mesh):
    return jax.shard_map(
        functools.partial(body, mesh.shape["wall"], mesh.shape["harm"]),
        mesh=mesh,
        in_specs=(
            P(("freq", "harm"), "wall", None),
            P(("freq", "harm"), "wall", None),
            P("freq", "wall", None),
            P("freq", "wall", None),
            P("freq"),
        ),
        out_specs=(P(("freq", "harm"), "wall", None), P("freq", None)),
        check_vma=False,
    )
```

```python
import functools

import jax
import jax.numpy as jnp
from jax import lax
from jax.experimental import pallas as pl
from jax.experimental.pallas import tpu as pltpu
from jax.sharding import PartitionSpec as P

BAND = 4
SWEEPS = 3
MESH = pl.DeviceIdType.MESH


def flip(index, bit):
    return index + bit - 2 * bit * (lax.div(index, bit) % 2)


def bits_of(count):
    return [1 << b for b in range(count.bit_length() - 1)]


STEPS = (
    ("solve mid", 2, 1),
    ("couple near", 0, 0),
    ("couple mid", 0, 0),
    ("solve far", 2, 1),
    ("couple far", 0, 0),
    ("solve mid", 3, 1),
    ("couple mid", 1, 0),
    ("solve near", 3, 1),
    ("solve far", 3, 1),
    ("couple far", 1, 0),
    ("couple mid", 2, 0),
    ("couple near", 2, 0),
    ("couple far", 2, 0),
    ("couple mid", 3, 0),
    ("correct", 0, 0),
    ("couple far", 3, 0),
    ("correct", 1, 0),
    ("solve near", 0, 0),
    ("solve mid", 0, 0),
    ("correct", 2, 0),
    ("solve near", 1, 0),
    ("solve far", 0, 0),
    ("solve mid", 1, 0),
    ("correct", 3, 0),
    ("solve far", 1, 0),
    ("solve near", 2, 0),
)


def steps_of(count):
    if count == 4:
        return STEPS
    names = ("couple near", "couple mid", "couple far", "correct", "solve near", "solve mid", "solve far")
    steps = [(name, c, 0) for name in names for c in range(count)]
    return tuple(step for step in steps if step[0] != "couple near" or step[1] == mate(step[1], count))


def mate(c, count):
    return c - c % 2 if count % 2 == 0 else c


def pack(full, packed):
    width = full.shape[0]
    part, quarter = width // 2, width // 4
    row = lax.broadcasted_iota(jnp.int32, (part, width), 0)
    lane = lax.broadcasted_iota(jnp.int32, (part, width), 1)
    left = lane[:quarter] < part
    top, low = full[:part], pltpu.roll(full[part:], part, 1)
    turned = pltpu.roll(top, part, 1)
    packed[0, :quarter] = jnp.where(left, turned[:quarter], top[quarter:])
    mixed = jnp.where(row <= lane, top, low)
    packed[1, :quarter] = jnp.where(left, mixed[:quarter], pltpu.roll(mixed[quarter:], part, 1))
    diagonal = jnp.sum(jnp.where(row == lane, low, 0.0), axis=0, keepdims=True)
    packed[0, quarter:] = jnp.zeros((8, width), jnp.float32)
    packed[1, quarter:] = jnp.broadcast_to(diagonal, (8, width))


def unpack(packed, width):
    part, quarter = width // 2, width // 4
    row = lax.broadcasted_iota(jnp.int32, (part, width), 0)
    lane = lax.broadcasted_iota(jnp.int32, (part, width), 1)
    cross, mixed = packed[0, :quarter], packed[1, :quarter]
    cross = jnp.concatenate([pltpu.roll(cross, part, 1), cross], axis=0)
    mixed = jnp.concatenate([mixed, pltpu.roll(mixed, part, 1)], axis=0)
    diagonal = jnp.broadcast_to(packed[1, quarter : quarter + 1], (part, width))
    top = jnp.where(lane < part, jnp.where(row <= lane, mixed, 0.0), cross)
    low = jnp.where(row > lane, mixed, jnp.where(row == lane, diagonal, 0.0))
    once = jnp.concatenate([top, pltpu.roll(low, part, 1)], axis=0)
    row = lax.broadcasted_iota(jnp.int32, (width, width), 0)
    lane = lax.broadcasted_iota(jnp.int32, (width, width), 1)
    return jnp.where(row == lane, once, once + once.T)


def sweep_kernel(
    walls, harms, strip_in, sketch, inverse, up, down, sampled, gram,
    strip, sampled_v, sketch_v, pieces, inverse_v, couple_v, solved, local, away, halo_out, halo_in,
    packed, summed, gathered, gram_out, gram_in,
    load_sem, recv_sem, send_sem, halo_send, halo_recv, gram_send, gram_recv, word,
):
    count, rows, width = sketch.shape
    lanes = width // count
    w = lax.axis_index("wall")
    z = lax.axis_index("harm")
    prev, following = (z + harms - 1) % harms, (z + 1) % harms
    wall_bits, harm_bits = bits_of(walls), bits_of(harms)
    lane = lax.broadcasted_iota(jnp.int32, (rows, width), 1)

    near = min(4, harms)
    butterfly = [("wall", flip(w, b)) for b in wall_bits if b > 2]
    butterfly += [("harm", flip(z, b)) for b in harm_bits if b >= near]
    greet = [{"wall": flip(w, b)} for b in wall_bits]
    greet += [{"harm": flip(z, b)} for b in harm_bits if b >= near]
    if harms < 3:
        greet += [{"harm": prev}, {"harm": following}]
    direct = []
    for across in range(2):
        for d in range(near):
            peer = {"harm": z - z % near + (z % near + d) % near} if d else {}
            peer.update({"wall": flip(w, 2)} if across else {})
            direct += [peer] if peer else []
    barrier = pltpu.get_barrier_semaphore()

    own_copy = pltpu.make_async_copy(sketch, sketch_v, load_sem.at[0])
    own_copy.start()
    strip_copy = pltpu.make_async_copy(strip_in, strip, load_sem.at[1 + 3 * walls])
    strip_copy.start()
    for peer in greet:
        pl.semaphore_signal(barrier, inc=1, device_id=peer, device_id_type=MESH)

    def tell(semaphore, peer):
        pl.semaphore_signal(semaphore, inc=1, device_id={"harm": peer}, device_id_type=MESH)

    heard = len(greet)
    if harms > 2:
        pl.when(z > 0)(lambda: tell(barrier, prev))
        pl.when(z < harms - 1)(lambda: tell(barrier, following))
        heard = heard + (z > 0).astype(jnp.int32) + (z < harms - 1).astype(jnp.int32)

    def first_word():
        pl.when(z == 1)(lambda: tell(word.at[0], following))
        pl.when(z == harms - 2)(lambda: tell(word.at[1], prev))

    def pass_on():
        @pl.when((z > 1) & (z < harms - 1))
        def _():
            pl.semaphore_wait(word.at[0], 1)
            tell(word.at[0], following)

        @pl.when((z > 0) & (z < harms - 2))
        def _():
            pl.semaphore_wait(word.at[1], 1)
            tell(word.at[1], prev)

    def last_word():
        pl.when(z == harms - 1)(lambda: pl.semaphore_wait(word.at[0], 1))
        pl.when(z == 0)(lambda: pl.semaphore_wait(word.at[1], 1))


    inverse_loads, couple_loads = [], []
    for m in range(walls):
        source = w
        for b in wall_bits:
            if m & b:
                source = flip(source, b)
        there = pl.ds(pl.multiple_of(source * rows, rows), rows)
        here = pl.ds(m * rows, rows)
        inverse_loads.append(pltpu.make_async_copy(
            inverse.at[:, :, there], inverse_v.at[:, :, here], load_sem.at[1 + m]
        ))
        for at, matrix in enumerate((up, down)):
            couple_loads.append(pltpu.make_async_copy(
                matrix.at[:, :, there], couple_v.at[at, :, :, here],
                load_sem.at[1 + walls * (1 + at) + m],
            ))
    for copy in inverse_loads + couple_loads:
        copy.start()

    def hop(g, c, m, bit):
        return pltpu.make_async_remote_copy(
            src_ref=pieces.at[g, c, m], dst_ref=pieces.at[g, c, m + bit],
            send_sem=send_sem.at[g, c, m + bit], recv_sem=recv_sem.at[g, c, m + bit],
            device_id={"wall": flip(w, bit)}, device_id_type=MESH,
        )

    def arrival(g, c, m):
        low = m & -m
        return hop(g, c, m - low, low)

    def send_own(g, c):
        for bit in reversed(wall_bits):
            hop(g, c, 0, bit).start()

    relayed = sorted(range(2, walls, 2), key=lambda m: -(m & -m))
    spans = {
        "near": [(0, min(2, walls))],
        "mid": [(m, m + 1) for m in range(2, walls, 2)],
        "far": [(m, m + 1) for m in range(3, walls, 2)],
    }

    def collect(part, g, c):
        if part == "near":
            if walls > 1:
                arrival(g, c, 1).wait_recv()
        elif part == "mid":
            for m in relayed:
                arrival(g, c, m).wait_recv()
                for bit in reversed(wall_bits):
                    if bit < (m & -m):
                        hop(g, c, m, bit).start()
        else:
            for m in range(3, walls, 2):
                arrival(g, c, m).wait_recv()

    def times(matrix, g, chunks, low, high):
        sides = [pieces[g, c, low:high].reshape((high - low) * rows, width) for c in chunks]
        piece = sides[0] if len(sides) == 1 else jnp.concatenate(sides, axis=1)
        return jnp.dot(
            matrix[:, low * rows : high * rows], piece, preferred_element_type=jnp.float32
        )

    def halo(s, side, c):
        return pltpu.make_async_remote_copy(
            src_ref=halo_out.at[s, side, c], dst_ref=halo_in.at[s, side, c],
            send_sem=halo_send.at[s, side, c], recv_sem=halo_recv.at[s, side, c],
            device_id={"harm": prev if side == 0 else following}, device_id_type=MESH,
        )

    def start(c):
        tile = None
        for h in range(count):
            turn = (h - c) % count * lanes
            source = sketch_v[h].astype(jnp.float32)
            source = source if turn == 0 else pltpu.roll(source, turn, 1)
            tile = source if tile is None else jnp.where(lane < h * lanes, tile, source)
        pieces[0, c, 0] = tile.astype(jnp.bfloat16)

    steps = steps_of(count)

    def opens(kind, part, c):
        place = {}
        for at, (name, chunk, lag) in enumerate(steps):
            place[name, chunk] = at + lag * len(steps)
        lead = mate(c, count) if kind == "couple" else c
        near_at, mid_at = place[kind + " near", lead], place[kind + " mid", c]
        return part != "far" and (near_at < mid_at) == (part == "near")

    def stays_of(side, shift):
        if side == 1:
            return lax.rem(shift, width), lane >= shift
        return width - shift, lane < width - shift

    def couple(part, s, c):
        g = 2 * s + 1
        chunks = [c]
        if part == "near" and count % 2 == 0:
            chunks = [c, c + 1]
        for chunk in chunks:
            collect(part, g, chunk)
        inner, outer = {}, {}
        for chunk in chunks:
            if opens("couple", part, chunk):
                inner[chunk] = pieces[0, chunk, 0].astype(jnp.float32)
            else:
                inner[chunk] = local[chunk]
        shifts = [(strip[j] + 1) * lanes for j in range(BAND)]
        for side in (1, 0):
            for chunk in chunks:
                if opens("couple", part, chunk):
                    outer[chunk] = jnp.zeros((rows, width), jnp.float32)
                else:
                    outer[chunk] = away[side, chunk]
            for j in range(BAND):
                turn, stays = stays_of(side, shifts[j])
                for low, high in spans[part]:
                    both = times(couple_v.at[1 - side, j], g, chunks, low, high)
                    for at, chunk in enumerate(chunks):
                        product = pltpu.roll(both[:, at * width : (at + 1) * width], turn, 1)
                        inner[chunk] = inner[chunk] - jnp.where(stays, product, 0.0)
                        outer[chunk] = outer[chunk] + jnp.where(stays, 0.0, product)
            for chunk in chunks:
                if part == "far":
                    halo_out[s, side, chunk] = outer[chunk].astype(jnp.bfloat16)
                    halo(s, side, chunk).start()
                else:
                    away[side, chunk] = outer[chunk]
        for chunk in chunks:
            local[chunk] = inner[chunk]

    def correct(s, c):
        rhs = local[c]
        for side in (1, 0):
            halo(s, side, c).wait_recv()
            rhs = rhs - halo_in[s, side, c].astype(jnp.float32)
        pieces[2 * s + 2, c, 0] = rhs.astype(jnp.bfloat16)
        send_own(2 * s + 2, c)

    def solve(part, s, c):
        g = 2 * s + 2
        collect(part, g, c)
        total = None
        for low, high in spans[part]:
            result = None
            for h in range(count):
                product = times(inverse_v.at[h], g, [c], low, high)
                result = product if result is None else jnp.where(lane < h * lanes, result, product)
            total = result if total is None else total + result
        if not opens("solve", part, c):
            total = solved[c] + total
        if part == "far":
            @pl.when(s < SWEEPS - 1)
            def _():
                pieces[g + 1, c, 0] = total.astype(jnp.bfloat16)
                send_own(g + 1, c)
        solved[c] = total

    def take(steps, s):
        for name, c, lag in steps:
            kind, _, part = name.partition(" ")
            if kind == "couple":
                couple(part, s, c)
            elif kind == "correct":
                correct(s, c)
            else:
                solve(part, s - lag, c)

    own_copy.wait()
    for c in range(count):
        start(c)
    pl.semaphore_wait(barrier, heard)
    for c in range(count):
        send_own(0, c)
    if harms > 2:
        first_word()
    strip_copy.wait()
    for copy in inverse_loads:
        copy.wait()
    if harms > 2:
        pass_on()
    solves = [step for step in steps if step[0].startswith("solve")]
    take([step for step in solves if step[2] == 0], -1)
    for copy in couple_loads:
        copy.wait()
    if harms > 2:
        last_word()
    pl.loop(0, SWEEPS)(lambda s: take(steps, s))
    take([step for step in solves if step[2] == 1], SWEEPS)

    out_copies = [
        pltpu.make_async_copy(sampled_v.at[h], sampled.at[h], load_sem.at[2 + 3 * walls + h])
        for h in range(count)
    ]
    total = jnp.zeros((width, width), jnp.float32)
    for h in range(count):
        tile = None
        for c in range(count):
            turn = (c - h) % count * lanes
            source = solved[c] if turn == 0 else pltpu.roll(solved[c], turn, 1)
            tile = source if tile is None else jnp.where(lane < c * lanes, tile, source)
        sampled_v[h] = tile
        out_copies[h].start()
        total = total + lax.dot_general(
            tile, tile, (((0,), (0,)), ((), ())),
            precision=lax.Precision.HIGHEST, preferred_element_type=jnp.float32,
        )

    def swap(stage, source, target, peer):
        copy = pltpu.make_async_remote_copy(
            src_ref=source, dst_ref=target, send_sem=gram_send.at[stage],
            recv_sem=gram_recv.at[stage], device_id=peer, device_id_type=MESH,
        )
        copy.start()
        return copy

    side = w % 2
    pack(total, packed)
    swap(0, packed.at[1 - side], gram_in.at[0], {"wall": flip(w, 1)}).wait()
    half = packed[side] + gram_in[0]
    stage = 1
    for axis, peer in butterfly:
        gram_out[stage] = half
        swap(stage, gram_out.at[stage], gram_in.at[stage], {axis: peer}).wait()
        half = half + gram_in[stage]
        stage += 1
    me = lax.div(w, 2) % 2 * near + z % near
    gathered[me] = half
    copies = [
        swap(stage + at, gathered.at[me], gathered.at[me], peer)
        for at, peer in enumerate(direct)
    ]
    for copy in out_copies:
        copy.wait()

    @pl.loop(0, 2 * SWEEPS + 1)
    def _(g):
        for c in range(count):
            for m in range(1, walls):
                arrival(g, c, m).wait_send()

    @pl.loop(0, SWEEPS)
    def _(s):
        for c in range(count):
            for side in range(2):
                halo(s, side, c).wait_send()

    for copy in copies:
        copy.wait()
    half = gathered[0]
    for slot in range(1, len(direct) + 1):
        half = half + gathered[slot]
    stage += len(direct)
    summed[side] = half / (harms * walls * count * rows)
    swap(stage, summed.at[side], summed.at[side], {"wall": flip(w, 1)}).wait()
    gram[...] = unpack(summed, width)


def factor_kernel(sampled, gram, basis, triangle, sampled_v, basis_v, work, inverse_lower, sems):
    count, rows, width = sampled_v.shape
    panel, block = 32, 16
    loads = [
        pltpu.make_async_copy(sampled.at[h], sampled_v.at[h], sems.at[0, h]) for h in range(count)
    ]
    stores = [pltpu.make_async_copy(basis_v.at[h], basis.at[h], sems.at[1, h]) for h in range(count)]
    for copy in loads:
        copy.start()
    row_at = lax.broadcasted_iota(jnp.int32, (width, width), 0)
    col_at = lax.broadcasted_iota(jnp.int32, (width, width), 1)
    at = lax.broadcasted_iota(jnp.int32, (panel, width), 0)
    work[...] = gram[...]
    inverse_lower[...] = jnp.where(row_at == col_at, 1.0, 0.0)

    def spread(value, i):
        return jnp.broadcast_to(value[i : i + 1, :], (panel, width))

    for low in range(0, width, panel):
        a = work[low : low + panel, :]
        x = inverse_lower[low : low + panel, :]
        pivots = jnp.ones((panel, width), jnp.float32)
        for first in range(0, panel, block):
            columns = {
                i: jnp.broadcast_to(a[:, low + i : low + i + 1], (panel, width))
                for i in range(first, first + block)
            }
            for i in range(first, first + block):
                pivot = spread(columns[i], i)
                pivots = jnp.where(at == i, pivot, pivots)
                factor = jnp.where(at > i, columns[i] * (1.0 / pivot), 0.0)
                for m in range(i + 1, first + block):
                    columns[m] = columns[m] - factor * spread(columns[m], i)
                a = a - factor * spread(a, i)
                x = x - factor * spread(x, i)
        unit = lax.rsqrt(pivots)
        a, x = a * unit, x * unit
        work[low : low + panel, :] = a
        inverse_lower[low : low + panel, :] = x
        if low + panel < width:
            change = lax.dot_general(
                a, jnp.concatenate([a, x], axis=1), (((0,), (0,)), ((), ())),
                precision=lax.Precision.HIGHEST, preferred_element_type=jnp.float32,
            )
            below = low + panel
            work[below:, :] = work[below:, :] - change[below:, :width]
            inverse_lower[below:, :] = inverse_lower[below:, :] - change[below:, width:]

    for h in range(count):
        loads[h].wait()
        basis_v[h] = lax.dot_general(
            sampled_v[h], inverse_lower[...], (((1,), (1,)), ((), ())),
            precision=lax.Precision.HIGHEST, preferred_element_type=jnp.float32,
        )
        stores[h].start()
    triangle[...] = jnp.where(row_at <= col_at, work[...], 0.0)
    for copy in stores:
        copy.wait()


def body(walls, harms, sketch, inverse_blocks, couple_up, couple_down, strip_harmonics):
    count, rows, width = sketch.shape
    size = rows * walls
    near = min(4, harms)
    stages = len(bits_of(walls)) + len(bits_of(harms // near)) + 2 * near
    short = width // 4 + 8
    gathers = 1 + 2 * SWEEPS
    vmem = pl.BlockSpec(memory_space=pltpu.VMEM)
    anywhere = pl.BlockSpec(memory_space=pl.ANY)
    sampled, gram = pl.pallas_call(
        functools.partial(sweep_kernel, walls, harms),
        out_shape=(
            jax.ShapeDtypeStruct((count, rows, width), jnp.float32),
            jax.ShapeDtypeStruct((width, width), jnp.float32),
        ),
        in_specs=[anywhere] * 5,
        out_specs=(anywhere, vmem),
        scratch_shapes=[
            pltpu.SMEM((BAND,), jnp.int32),
            pltpu.VMEM((count, rows, width), jnp.float32),
            pltpu.VMEM((count, rows, width), jnp.bfloat16),
            pltpu.VMEM((gathers, count, walls, rows, width), jnp.bfloat16),
            pltpu.VMEM((count, rows, size), jnp.bfloat16),
            pltpu.VMEM((2, BAND, rows, size), jnp.bfloat16),
            pltpu.VMEM((count, rows, width), jnp.float32),
            pltpu.VMEM((count, rows, width), jnp.float32),
            pltpu.VMEM((2, count, rows, width), jnp.float32),
            pltpu.VMEM((SWEEPS, 2, count, rows, width), jnp.bfloat16),
            pltpu.VMEM((SWEEPS, 2, count, rows, width), jnp.bfloat16),
            pltpu.VMEM((2, short, width), jnp.float32),
            pltpu.VMEM((2, short, width), jnp.float32),
            pltpu.VMEM((2 * near, short, width), jnp.float32),
            pltpu.VMEM((stages, short, width), jnp.float32),
            pltpu.VMEM((stages, short, width), jnp.float32),
            pltpu.SemaphoreType.DMA((2 + 3 * walls + count,)),
            pltpu.SemaphoreType.DMA((gathers, count, walls)),
            pltpu.SemaphoreType.DMA((gathers, count, walls)),
            pltpu.SemaphoreType.DMA((SWEEPS, 2, count)),
            pltpu.SemaphoreType.DMA((SWEEPS, 2, count)),
            pltpu.SemaphoreType.DMA((stages,)),
            pltpu.SemaphoreType.DMA((stages,)),
            pltpu.SemaphoreType.REGULAR((2,)),
        ],
        compiler_params=pltpu.CompilerParams(
            collective_id=0, has_side_effects=True, vmem_limit_bytes=67043328
        ),
        name="sweeps",
    )(strip_harmonics, sketch, inverse_blocks, couple_up, couple_down)
    return pl.pallas_call(
        factor_kernel,
        out_shape=(
            jax.ShapeDtypeStruct((count, rows, width), jnp.float32),
            jax.ShapeDtypeStruct((width, width), jnp.float32),
        ),
        in_specs=[anywhere, vmem],
        out_specs=(anywhere, vmem),
        scratch_shapes=[
            pltpu.VMEM((count, rows, width), jnp.float32),
            pltpu.VMEM((count, rows, width), jnp.float32),
            pltpu.VMEM((width, width), jnp.float32),
            pltpu.VMEM((width, width), jnp.float32),
            pltpu.SemaphoreType.DMA((2, count)),
        ],
        compiler_params=pltpu.CompilerParams(),
        name="factor",
    )(sampled, gram)


def solution(mesh):
    return jax.shard_map(
        functools.partial(body, mesh.shape["wall"], mesh.shape["harm"]),
        mesh=mesh,
        in_specs=(
            P(("freq", "harm"), "wall", None),
            P(("freq", "harm"), "wall", None),
            P("freq", "wall", None),
            P("freq", "wall", None),
            P("freq"),
        ),
        out_specs=(P(("freq", "harm"), "wall", None), P("freq", None)),
        check_vma=False,
    )
```

```python
import functools

import jax
import jax.numpy as jnp
from jax import lax
from jax.experimental import pallas as pl
from jax.experimental.pallas import tpu as pltpu
from jax.sharding import PartitionSpec as P

BAND = 4
SWEEPS = 3
MESH = pl.DeviceIdType.MESH


def flip(index, bit):
    return index + bit - 2 * bit * (lax.div(index, bit) % 2)


def bits_of(count):
    return [1 << b for b in range(count.bit_length() - 1)]


STEPS = (
    ("solve mid", 2, 1),
    ("couple near", 0, 0),
    ("couple mid", 0, 0),
    ("solve far", 2, 1),
    ("couple far", 0, 0),
    ("solve mid", 3, 1),
    ("couple mid", 1, 0),
    ("solve near", 3, 1),
    ("solve far", 3, 1),
    ("couple far", 1, 0),
    ("couple mid", 2, 0),
    ("couple near", 2, 0),
    ("couple far", 2, 0),
    ("couple mid", 3, 0),
    ("correct", 0, 0),
    ("couple far", 3, 0),
    ("correct", 1, 0),
    ("solve near", 0, 0),
    ("solve mid", 0, 0),
    ("correct", 2, 0),
    ("solve near", 1, 0),
    ("solve far", 0, 0),
    ("solve mid", 1, 0),
    ("correct", 3, 0),
    ("solve far", 1, 0),
    ("solve near", 2, 0),
)


def steps_of(count):
    if count == 4:
        return STEPS
    names = ("couple near", "couple mid", "couple far", "correct", "solve near", "solve mid", "solve far")
    steps = [(name, c, 0) for name in names for c in range(count)]
    return tuple(step for step in steps if step[0] != "couple near" or step[1] == mate(step[1], count))


def mate(c, count):
    return c - c % 2 if count % 2 == 0 else c


def pack(full, packed):
    width = full.shape[0]
    part, quarter = width // 2, width // 4
    row = lax.broadcasted_iota(jnp.int32, (part, width), 0)
    lane = lax.broadcasted_iota(jnp.int32, (part, width), 1)
    left = lane[:quarter] < part
    top, low = full[:part], pltpu.roll(full[part:], part, 1)
    turned = pltpu.roll(top, part, 1)
    packed[0, :quarter] = jnp.where(left, turned[:quarter], top[quarter:])
    mixed = jnp.where(row <= lane, top, low)
    packed[1, :quarter] = jnp.where(left, mixed[:quarter], pltpu.roll(mixed[quarter:], part, 1))
    diagonal = jnp.sum(jnp.where(row == lane, low, 0.0), axis=0, keepdims=True)
    packed[0, quarter:] = jnp.zeros((8, width), jnp.float32)
    packed[1, quarter:] = jnp.broadcast_to(diagonal, (8, width))


def unpack(packed, width):
    part, quarter = width // 2, width // 4
    row = lax.broadcasted_iota(jnp.int32, (part, width), 0)
    lane = lax.broadcasted_iota(jnp.int32, (part, width), 1)
    cross, mixed = packed[0, :quarter], packed[1, :quarter]
    cross = jnp.concatenate([pltpu.roll(cross, part, 1), cross], axis=0)
    mixed = jnp.concatenate([mixed, pltpu.roll(mixed, part, 1)], axis=0)
    diagonal = jnp.broadcast_to(packed[1, quarter : quarter + 1], (part, width))
    top = jnp.where(lane < part, jnp.where(row <= lane, mixed, 0.0), cross)
    low = jnp.where(row > lane, mixed, jnp.where(row == lane, diagonal, 0.0))
    once = jnp.concatenate([top, pltpu.roll(low, part, 1)], axis=0)
    row = lax.broadcasted_iota(jnp.int32, (width, width), 0)
    lane = lax.broadcasted_iota(jnp.int32, (width, width), 1)
    return jnp.where(row == lane, once, once + once.T)


def sweep_kernel(
    walls, harms, strip_in, sketch, inverse, up, down, sampled, gram,
    strip, sampled_v, sketch_v, pieces, inverse_v, couple_v, solved, local, away, halo_out, halo_in,
    packed, summed, gathered, gram_out, gram_in,
    load_sem, recv_sem, send_sem, halo_send, halo_recv, gram_send, gram_recv, word,
):
    count, rows, width = sketch.shape
    lanes = width // count
    w = lax.axis_index("wall")
    z = lax.axis_index("harm")
    prev, following = (z + harms - 1) % harms, (z + 1) % harms
    wall_bits, harm_bits = bits_of(walls), bits_of(harms)
    lane = lax.broadcasted_iota(jnp.int32, (rows, width), 1)

    near = min(4, harms)
    butterfly = [("wall", flip(w, b)) for b in wall_bits if b > 2]
    butterfly += [("harm", flip(z, b)) for b in harm_bits if b >= near]
    greet = [{"wall": flip(w, b)} for b in wall_bits]
    greet += [{"harm": flip(z, b)} for b in harm_bits if b >= near]
    if harms < 3:
        greet += [{"harm": prev}, {"harm": following}]
    direct = []
    for across in range(2):
        for d in range(near):
            peer = {"harm": z - z % near + (z % near + d) % near} if d else {}
            peer.update({"wall": flip(w, 2)} if across else {})
            direct += [peer] if peer else []
    barrier = pltpu.get_barrier_semaphore()

    own_copy = pltpu.make_async_copy(sketch, sketch_v, load_sem.at[0])
    own_copy.start()
    strip_copy = pltpu.make_async_copy(strip_in, strip, load_sem.at[1 + 3 * walls])
    strip_copy.start()
    for peer in greet:
        pl.semaphore_signal(barrier, inc=1, device_id=peer, device_id_type=MESH)

    def tell(semaphore, peer):
        pl.semaphore_signal(semaphore, inc=1, device_id={"harm": peer}, device_id_type=MESH)

    heard = len(greet)
    if harms > 2:
        pl.when(z > 0)(lambda: tell(barrier, prev))
        pl.when(z < harms - 1)(lambda: tell(barrier, following))
        heard = heard + (z > 0).astype(jnp.int32) + (z < harms - 1).astype(jnp.int32)

    def first_word():
        pl.when(z == 1)(lambda: tell(word.at[0], following))
        pl.when(z == harms - 2)(lambda: tell(word.at[1], prev))

    def pass_on():
        @pl.when((z > 1) & (z < harms - 1))
        def _():
            pl.semaphore_wait(word.at[0], 1)
            tell(word.at[0], following)

        @pl.when((z > 0) & (z < harms - 2))
        def _():
            pl.semaphore_wait(word.at[1], 1)
            tell(word.at[1], prev)

    def last_word():
        pl.when(z == harms - 1)(lambda: pl.semaphore_wait(word.at[0], 1))
        pl.when(z == 0)(lambda: pl.semaphore_wait(word.at[1], 1))


    inverse_loads, couple_loads = [], []
    for m in range(walls):
        source = w
        for b in wall_bits:
            if m & b:
                source = flip(source, b)
        there = pl.ds(pl.multiple_of(source * rows, rows), rows)
        here = pl.ds(m * rows, rows)
        inverse_loads.append(pltpu.make_async_copy(
            inverse.at[:, :, there], inverse_v.at[:, :, here], load_sem.at[1 + m]
        ))
        for at, matrix in enumerate((up, down)):
            couple_loads.append(pltpu.make_async_copy(
                matrix.at[:, :, there], couple_v.at[at, :, :, here],
                load_sem.at[1 + walls * (1 + at) + m],
            ))
    for copy in inverse_loads + couple_loads:
        copy.start()

    def hop(g, c, m, bit):
        return pltpu.make_async_remote_copy(
            src_ref=pieces.at[g, c, m], dst_ref=pieces.at[g, c, m + bit],
            send_sem=send_sem.at[g, c, m + bit], recv_sem=recv_sem.at[g, c, m + bit],
            device_id={"wall": flip(w, bit)}, device_id_type=MESH,
        )

    def arrival(g, c, m):
        low = m & -m
        return hop(g, c, m - low, low)

    def send_own(g, c):
        for bit in reversed(wall_bits):
            hop(g, c, 0, bit).start()

    relayed = sorted(range(2, walls, 2), key=lambda m: -(m & -m))
    spans = {
        "near": [(0, min(2, walls))],
        "mid": [(m, m + 1) for m in range(2, walls, 2)],
        "far": [(m, m + 1) for m in range(3, walls, 2)],
    }

    def collect(part, g, c):
        if part == "near":
            if walls > 1:
                arrival(g, c, 1).wait_recv()
        elif part == "mid":
            for m in relayed:
                arrival(g, c, m).wait_recv()
                for bit in reversed(wall_bits):
                    if bit < (m & -m):
                        hop(g, c, m, bit).start()
        else:
            for m in range(3, walls, 2):
                arrival(g, c, m).wait_recv()

    def times(matrix, g, chunks, low, high):
        sides = [pieces[g, c, low:high].reshape((high - low) * rows, width) for c in chunks]
        piece = sides[0] if len(sides) == 1 else jnp.concatenate(sides, axis=1)
        return jnp.dot(
            matrix[:, low * rows : high * rows], piece, preferred_element_type=jnp.float32
        )

    def halo(s, side, c):
        return pltpu.make_async_remote_copy(
            src_ref=halo_out.at[s, side, c], dst_ref=halo_in.at[s, side, c],
            send_sem=halo_send.at[s, side, c], recv_sem=halo_recv.at[s, side, c],
            device_id={"harm": prev if side == 0 else following}, device_id_type=MESH,
        )

    def start(c):
        tile = None
        for h in range(count):
            turn = (h - c) % count * lanes
            source = sketch_v[h].astype(jnp.float32)
            source = source if turn == 0 else pltpu.roll(source, turn, 1)
            tile = source if tile is None else jnp.where(lane < h * lanes, tile, source)
        pieces[0, c, 0] = tile.astype(jnp.bfloat16)

    steps = steps_of(count)

    def opens(kind, part, c):
        place = {}
        for at, (name, chunk, lag) in enumerate(steps):
            place[name, chunk] = at + lag * len(steps)
        lead = mate(c, count) if kind == "couple" else c
        near_at, mid_at = place[kind + " near", lead], place[kind + " mid", c]
        return part != "far" and (near_at < mid_at) == (part == "near")

    def stays_of(side, shift):
        if side == 1:
            return lax.rem(shift, width), lane >= shift
        return width - shift, lane < width - shift

    def couple(part, s, c):
        g = 2 * s + 1
        chunks = [c]
        if part == "near" and count % 2 == 0:
            chunks = [c, c + 1]
        for chunk in chunks:
            collect(part, g, chunk)
        inner, outer = {}, {}
        for chunk in chunks:
            if opens("couple", part, chunk):
                inner[chunk] = pieces[0, chunk, 0].astype(jnp.float32)
            else:
                inner[chunk] = local[chunk]
        shifts = [(strip[j] + 1) * lanes for j in range(BAND)]
        for side in (1, 0):
            for chunk in chunks:
                if opens("couple", part, chunk):
                    outer[chunk] = jnp.zeros((rows, width), jnp.float32)
                else:
                    outer[chunk] = away[side, chunk]
            for j in range(BAND):
                turn, stays = stays_of(side, shifts[j])
                for low, high in spans[part]:
                    both = times(couple_v.at[1 - side, j], g, chunks, low, high)
                    for at, chunk in enumerate(chunks):
                        product = pltpu.roll(both[:, at * width : (at + 1) * width], turn, 1)
                        inner[chunk] = inner[chunk] - jnp.where(stays, product, 0.0)
                        outer[chunk] = outer[chunk] + jnp.where(stays, 0.0, product)
            for chunk in chunks:
                if part == "far":
                    halo_out[s, side, chunk] = outer[chunk].astype(jnp.bfloat16)
                    halo(s, side, chunk).start()
                else:
                    away[side, chunk] = outer[chunk]
        for chunk in chunks:
            local[chunk] = inner[chunk]

    def correct(s, c):
        rhs = local[c]
        for side in (1, 0):
            halo(s, side, c).wait_recv()
            rhs = rhs - halo_in[s, side, c].astype(jnp.float32)
        pieces[2 * s + 2, c, 0] = rhs.astype(jnp.bfloat16)
        send_own(2 * s + 2, c)

    def solve(part, s, c):
        g = 2 * s + 2
        collect(part, g, c)
        total = None
        for low, high in spans[part]:
            result = None
            for h in range(count):
                product = times(inverse_v.at[h], g, [c], low, high)
                result = product if result is None else jnp.where(lane < h * lanes, result, product)
            total = result if total is None else total + result
        if not opens("solve", part, c):
            total = solved[c] + total
        if part == "far":
            @pl.when(s < SWEEPS - 1)
            def _():
                pieces[g + 1, c, 0] = total.astype(jnp.bfloat16)
                send_own(g + 1, c)
        solved[c] = total

    def take(steps, s):
        for name, c, lag in steps:
            kind, _, part = name.partition(" ")
            if kind == "couple":
                couple(part, s, c)
            elif kind == "correct":
                correct(s, c)
            else:
                solve(part, s - lag, c)

    own_copy.wait()
    for c in range(count):
        start(c)
    pl.semaphore_wait(barrier, heard)
    for c in range(count):
        send_own(0, c)
    if harms > 2:
        first_word()
    strip_copy.wait()
    for copy in inverse_loads:
        copy.wait()
    if harms > 2:
        pass_on()
    solves = [step for step in steps if step[0].startswith("solve")]
    take([step for step in solves if step[2] == 0], -1)
    for copy in couple_loads:
        copy.wait()
    if harms > 2:
        last_word()
    pl.loop(0, SWEEPS)(lambda s: take(steps, s))
    take([step for step in solves if step[2] == 1], SWEEPS)

    out_copies = [
        pltpu.make_async_copy(sampled_v.at[h], sampled.at[h], load_sem.at[2 + 3 * walls + h])
        for h in range(count)
    ]
    for h in range(count):
        tile = None
        for c in range(count):
            turn = (c - h) % count * lanes
            source = solved[c] if turn == 0 else pltpu.roll(solved[c], turn, 1)
            tile = source if tile is None else jnp.where(lane < c * lanes, tile, source)
        sampled_v[h] = tile
        out_copies[h].start()
    flat = sampled_v[...].reshape(count * rows, width)
    total = lax.dot_general(
        flat, flat, (((0,), (0,)), ((), ())),
        precision=lax.Precision.HIGHEST, preferred_element_type=jnp.float32,
    )

    def swap(stage, source, target, peer):
        copy = pltpu.make_async_remote_copy(
            src_ref=source, dst_ref=target, send_sem=gram_send.at[stage],
            recv_sem=gram_recv.at[stage], device_id=peer, device_id_type=MESH,
        )
        copy.start()
        return copy

    side = w % 2
    pack(total, packed)
    swap(0, packed.at[1 - side], gram_in.at[0], {"wall": flip(w, 1)}).wait()
    half = packed[side] + gram_in[0]
    stage = 1
    for axis, peer in butterfly:
        gram_out[stage] = half
        swap(stage, gram_out.at[stage], gram_in.at[stage], {axis: peer}).wait()
        half = half + gram_in[stage]
        stage += 1
    me = lax.div(w, 2) % 2 * near + z % near
    gathered[me] = half
    copies = [
        swap(stage + at, gathered.at[me], gathered.at[me], peer)
        for at, peer in enumerate(direct)
    ]
    for copy in out_copies:
        copy.wait()

    @pl.loop(0, 2 * SWEEPS + 1)
    def _(g):
        for c in range(count):
            for m in range(1, walls):
                arrival(g, c, m).wait_send()

    @pl.loop(0, SWEEPS)
    def _(s):
        for c in range(count):
            for side in range(2):
                halo(s, side, c).wait_send()

    for copy in copies:
        copy.wait()
    half = gathered[0]
    for slot in range(1, len(direct) + 1):
        half = half + gathered[slot]
    stage += len(direct)
    summed[side] = half / (harms * walls * count * rows)
    swap(stage, summed.at[side], summed.at[side], {"wall": flip(w, 1)}).wait()
    gram[...] = unpack(summed, width)


def factor_kernel(sampled, gram, basis, triangle, sampled_v, basis_v, work, inverse_lower, sems):
    count, rows, width = sampled_v.shape
    panel, block = 32, 16
    loads = [
        pltpu.make_async_copy(sampled.at[h], sampled_v.at[h], sems.at[0, h]) for h in range(count)
    ]
    stores = [pltpu.make_async_copy(basis_v.at[h], basis.at[h], sems.at[1, h]) for h in range(count)]
    for copy in loads:
        copy.start()
    row_at = lax.broadcasted_iota(jnp.int32, (width, width), 0)
    col_at = lax.broadcasted_iota(jnp.int32, (width, width), 1)
    at = lax.broadcasted_iota(jnp.int32, (panel, width), 0)
    work[...] = gram[...]
    inverse_lower[...] = jnp.where(row_at == col_at, 1.0, 0.0)

    def spread(value, i):
        return jnp.broadcast_to(value[i : i + 1, :], (panel, width))

    for low in range(0, width, panel):
        a = work[low : low + panel, :]
        x = inverse_lower[low : low + panel, :]
        pivots = jnp.ones((panel, width), jnp.float32)
        for first in range(0, panel, block):
            columns = {
                i: jnp.broadcast_to(a[:, low + i : low + i + 1], (panel, width))
                for i in range(first, first + block)
            }
            for i in range(first, first + block):
                pivot = spread(columns[i], i)
                pivots = jnp.where(at == i, pivot, pivots)
                factor = jnp.where(at > i, columns[i] * (1.0 / pivot), 0.0)
                for m in range(i + 1, first + block):
                    columns[m] = columns[m] - factor * spread(columns[m], i)
                a = a - factor * spread(a, i)
                x = x - factor * spread(x, i)
        unit = lax.rsqrt(pivots)
        a, x = a * unit, x * unit
        work[low : low + panel, :] = a
        inverse_lower[low : low + panel, :] = x
        if low + panel < width:
            change = lax.dot_general(
                a, jnp.concatenate([a, x], axis=1), (((0,), (0,)), ((), ())),
                precision=lax.Precision.HIGHEST, preferred_element_type=jnp.float32,
            )
            below = low + panel
            work[below:, :] = work[below:, :] - change[below:, :width]
            inverse_lower[below:, :] = inverse_lower[below:, :] - change[below:, width:]

    for h in range(count):
        loads[h].wait()
        basis_v[h] = lax.dot_general(
            sampled_v[h], inverse_lower[...], (((1,), (1,)), ((), ())),
            precision=lax.Precision.HIGHEST, preferred_element_type=jnp.float32,
        )
        stores[h].start()
    triangle[...] = jnp.where(row_at <= col_at, work[...], 0.0)
    for copy in stores:
        copy.wait()


def body(walls, harms, sketch, inverse_blocks, couple_up, couple_down, strip_harmonics):
    count, rows, width = sketch.shape
    size = rows * walls
    near = min(4, harms)
    stages = len(bits_of(walls)) + len(bits_of(harms // near)) + 2 * near
    short = width // 4 + 8
    gathers = 1 + 2 * SWEEPS
    vmem = pl.BlockSpec(memory_space=pltpu.VMEM)
    anywhere = pl.BlockSpec(memory_space=pl.ANY)
    sampled, gram = pl.pallas_call(
        functools.partial(sweep_kernel, walls, harms),
        out_shape=(
            jax.ShapeDtypeStruct((count, rows, width), jnp.float32),
            jax.ShapeDtypeStruct((width, width), jnp.float32),
        ),
        in_specs=[anywhere] * 5,
        out_specs=(anywhere, vmem),
        scratch_shapes=[
            pltpu.SMEM((BAND,), jnp.int32),
            pltpu.VMEM((count, rows, width), jnp.float32),
            pltpu.VMEM((count, rows, width), jnp.bfloat16),
            pltpu.VMEM((gathers, count, walls, rows, width), jnp.bfloat16),
            pltpu.VMEM((count, rows, size), jnp.bfloat16),
            pltpu.VMEM((2, BAND, rows, size), jnp.bfloat16),
            pltpu.VMEM((count, rows, width), jnp.float32),
            pltpu.VMEM((count, rows, width), jnp.float32),
            pltpu.VMEM((2, count, rows, width), jnp.float32),
            pltpu.VMEM((SWEEPS, 2, count, rows, width), jnp.bfloat16),
            pltpu.VMEM((SWEEPS, 2, count, rows, width), jnp.bfloat16),
            pltpu.VMEM((2, short, width), jnp.float32),
            pltpu.VMEM((2, short, width), jnp.float32),
            pltpu.VMEM((2 * near, short, width), jnp.float32),
            pltpu.VMEM((stages, short, width), jnp.float32),
            pltpu.VMEM((stages, short, width), jnp.float32),
            pltpu.SemaphoreType.DMA((2 + 3 * walls + count,)),
            pltpu.SemaphoreType.DMA((gathers, count, walls)),
            pltpu.SemaphoreType.DMA((gathers, count, walls)),
            pltpu.SemaphoreType.DMA((SWEEPS, 2, count)),
            pltpu.SemaphoreType.DMA((SWEEPS, 2, count)),
            pltpu.SemaphoreType.DMA((stages,)),
            pltpu.SemaphoreType.DMA((stages,)),
            pltpu.SemaphoreType.REGULAR((2,)),
        ],
        compiler_params=pltpu.CompilerParams(
            collective_id=0, has_side_effects=True, vmem_limit_bytes=67043328
        ),
        name="sweeps",
    )(strip_harmonics, sketch, inverse_blocks, couple_up, couple_down)
    return pl.pallas_call(
        factor_kernel,
        out_shape=(
            jax.ShapeDtypeStruct((count, rows, width), jnp.float32),
            jax.ShapeDtypeStruct((width, width), jnp.float32),
        ),
        in_specs=[anywhere, vmem],
        out_specs=(anywhere, vmem),
        scratch_shapes=[
            pltpu.VMEM((count, rows, width), jnp.float32),
            pltpu.VMEM((count, rows, width), jnp.float32),
            pltpu.VMEM((width, width), jnp.float32),
            pltpu.VMEM((width, width), jnp.float32),
            pltpu.SemaphoreType.DMA((2, count)),
        ],
        compiler_params=pltpu.CompilerParams(),
        name="factor",
    )(sampled, gram)


def solution(mesh):
    return jax.shard_map(
        functools.partial(body, mesh.shape["wall"], mesh.shape["harm"]),
        mesh=mesh,
        in_specs=(
            P(("freq", "harm"), "wall", None),
            P(("freq", "harm"), "wall", None),
            P("freq", "wall", None),
            P("freq", "wall", None),
            P("freq"),
        ),
        out_specs=(P(("freq", "harm"), "wall", None), P("freq", None)),
        check_vma=False,
    )
```
